32 devices in a mesh: samp: 8 (over y, x, core), ctr: 4 (over z).
Axes of the slice: x: 2, y: 2, z: 4, core: 2. Of those that a mesh axis runs over, the one named last changes fastest.
Arguments:
- samples: bfloat16 [16384, 512], P('samp'), may hold values from -6 to 6
- centers: bfloat16 [4096, 512], P('ctr'), may hold values from -6 to 6
Outputs:
- gram_panel: float32 [4, 1024, 512], P('ctr', 'samp')
- chol_panel: float32 [4, 1024, 512], P('ctr', 'samp')
- precond_factor: float32 [512, 512], replicated
The draws below stay inside these ranges and needn't reach their ends.
All inputs are finite; a program needn't handle non-finite values.
Results may differ from the reference program's by a relative error of at most 0.0003.
Values may be sent and summed in bfloat16 or wider, within the bound.
No kernel may reach another device: no remote copies, remote signals or barrier semaphores. Data moves between devices by JAX's collectives and lax.ppermute only.
A program may use at most 64 MiB of HBM per device.

```python
import math
import jax
import jax.numpy as jnp
from jax import lax

D = 512
MC_DEV = 1024
PANEL = 512
M = 4096
NSAMP = 16384
N_CTR = 4


def group_centroids(key):
    group_count = 256
    centroid_key = jax.random.fold_in(key, 7)
    radius_key = jax.random.fold_in(key, 8)
    direction = jax.random.normal(centroid_key, (group_count, D), jnp.float32)
    log_radius = jax.random.uniform(radius_key, (group_count, 1), jnp.float32, math.log(0.2), math.log(1.0))
    return direction * jnp.exp(log_radius)


def grouped_points(key, point_count, offset):
    centroids = group_centroids(key)
    membership = jax.random.randint(jax.random.fold_in(key, offset), (point_count,), 0, 256)
    deviation_key = jax.random.fold_in(key, offset + 1)
    spread_key = jax.random.fold_in(key, offset + 2)
    deviation = jax.random.normal(deviation_key, (point_count, D), jnp.float32)
    log_spread = jax.random.uniform(spread_key, (point_count, 1), jnp.float32, math.log(0.5), math.log(1.0))
    points = jnp.take(centroids, membership, axis=0) + jnp.exp(log_spread) * deviation
    return jnp.clip(points, -6.0, 6.0).astype(jnp.bfloat16)


def draw_samples(key, part):
    return grouped_points(key, NSAMP, 11)


def draw_centers(key, part):
    return grouped_points(key, M, 21)


def setup_inputs(seed: int = 0) -> dict:
    streams_of = jax.random.split(jax.random.key(seed), 3)
    samples = draw_samples(jax.random.fold_in(streams_of[2], 71), 0)
    centers = draw_centers(jax.random.fold_in(streams_of[2], 71), 0)
    return {"samples": samples, "centers": centers}


JITTER_DIAG = 0.01
RIDGE_SHIFT = 0.5
GRAM_SCALE = 64.0

def kernel_block(first_set, second_set):
    cross_dot = lax.dot_general(first_set.astype(jnp.float32), second_set.astype(jnp.float32), (((1,), (1,)), ((), ())), preferred_element_type=jnp.float32)
    first_sq = jnp.sum(jnp.square(first_set.astype(jnp.float32)), axis=1)
    second_sq = jnp.sum(jnp.square(second_set.astype(jnp.float32)), axis=1)
    sq_dist = jnp.maximum(first_sq[:, None] + second_sq[None, :] - 2.0 * cross_dot, 0.0)
    return jnp.exp(-(2.0 / D) * sq_dist)

def reference(samples, centers):
    panel_centers = centers[:PANEL]
    kern_panel = kernel_block(samples, panel_centers).astype(jnp.bfloat16)
    center_blocks = centers.reshape(N_CTR, MC_DEV, D)

    def per_block(center_block):
        kern_block = kernel_block(samples, center_block).astype(jnp.bfloat16)
        return lax.dot_general(kern_block.astype(jnp.float32), kern_panel.astype(jnp.float32), (((0,), (0,)), ((), ())), preferred_element_type=jnp.float32)
    gram_panel = lax.map(per_block, center_blocks) * (GRAM_SCALE / NSAMP)
    identity = jnp.eye(PANEL, dtype=jnp.float32)
    center_panel = kernel_block(centers, panel_centers)
    shifted = jnp.concatenate([center_panel[:PANEL] + JITTER_DIAG * identity, center_panel[PANEL:]], axis=0)
    factor_low = jnp.linalg.cholesky(shifted[:PANEL])
    solved = lax.linalg.triangular_solve(factor_low, shifted, left_side=False, lower=True, transpose_a=True)
    chol_panel = solved.reshape(N_CTR, MC_DEV, PANEL)
    inner_gram = jnp.dot(factor_low.T, factor_low, precision=lax.Precision.HIGHEST) + RIDGE_SHIFT * identity
    precond_factor = jnp.linalg.cholesky(inner_gram)
    return (gram_panel, chol_panel, precond_factor)
```

```python
import functools
import jax, jax.numpy as jnp
from jax import lax
from jax.experimental import pallas as pl
from jax.experimental.pallas import tpu as pltpu
JITTER=0.01; SHIFT=0.5
B=128
VB=64
HI=lax.Precision.HIGHEST
def mmul(a,b): return jnp.dot(a,b,preferred_element_type=jnp.float32,precision=HI)
def mmul_nt(a,b): return lax.dot_general(a,b,(((1,),(1,)),((),())),preferred_element_type=jnp.float32,precision=HI)
def lanebc(x,c): return jnp.broadcast_to(x[:,c:c+1],(8,B))
def subbc(x,j): return jnp.broadcast_to(x[j:j+1,:],(8,B))

def factor128(r_ref,w_ref,u_ref,m_ref):
    row=lax.broadcasted_iota(jnp.int32,(B,B),0)
    lane=lax.broadcasted_iota(jnp.int32,(B,B),1)
    w_ref[...]=jnp.where(lane==row,1.0,0.0)
    n=VB//8
    for b in range(B//VB):
        base=b*VB
        X=[r_ref[base+8*k:base+8*k+8,:] for k in range(n)]
        Y=[w_ref[base+8*k:base+8*k+8,:] for k in range(n)]
        for i in range(n):
            a=X[i]; w=Y[i]
            g=[];c={m:[] for m in range(i+1,n)}
            for j in range(8):
                g.append(lanebc(a,base+8*i+j))
                for m in range(i+1,n): c[m].append(lanebc(X[m],base+8*i+j))
            for j in range(8):
                rs=lax.rsqrt(subbc(g[j],j))
                q=[None]*8
                lj=g[j]*rs
                for m in range(j+1,8):
                    q[m]=subbc(g[m],j)*rs
                    g[m]=g[m]-lj*q[m]
                ur=subbc(a,j)*rs; wr=subbc(w,j)*rs
                if j<7:
                    a=a-lj*ur; w=w-lj*wr
                k=base+8*i+j
                u_ref[k:k+1,:]=ur[0:1]; m_ref[k:k+1,:]=wr[0:1]
                for m in range(i+1,n):
                    cj=c[m][j]*rs
                    for t in range(j+1,8): c[m][t]=c[m][t]-cj*q[t]
                    X[m]=X[m]-cj*ur; Y[m]=Y[m]-cj*wr
        e=base+VB
        if e<B:
            ub=u_ref[base:e,:]; mb=m_ref[base:e,:]
            ut=ub.T[e:,:]
            z=mmul(ut,jnp.concatenate([ub,mb],axis=1))
            r_ref[e:,:]=r_ref[e:,:]-z[:,:B]
            w_ref[e:,:]=w_ref[e:,:]-z[:,B:]
    u_ref[...]=jnp.where(lane>=row,u_ref[...],0.0)

def kern_init(off_ref,panel_ref,own_ref,a_ref,nb,no):
    pan=panel_ref[...]; ow=own_ref[...]
    def bdot(a,b): return lax.dot_general(a,b,(((1,),(1,)),((),())),preferred_element_type=jnp.float32)
    c=-(2.0/panel_ref.shape[1])
    eye=lax.broadcasted_iota(jnp.int32,(B,B),0)==lax.broadcasted_iota(jnp.int32,(B,B),1)
    def diagrow(x):
        d=jnp.where(eye,x,0.0)
        return jnp.sum(d,axis=0,keepdims=True), jnp.sum(d,axis=1,keepdims=True)
    rows=[];cols=[]
    for i in range(nb):
        pi=pan[i*B:(i+1)*B]
        r,cc=diagrow(bdot(pi,pi)); rows.append(r); cols.append(cc)
    for i in range(no):
        oi=ow[i*B:(i+1)*B]
        r,_=diagrow(bdot(oi,oi)); rows.append(r)
    for i in range(nb):
        for j in range(i,nb+no):
            rhs=pan[j*B:(j+1)*B] if j<nb else ow[(j-nb)*B:(j-nb+1)*B]
            x=bdot(pan[i*B:(i+1)*B],rhs)
            k=jnp.exp(c*jnp.maximum(cols[i]+rows[j]-2.0*x,0.0))
            if j<nb:
                if i==j: k=k+jnp.where(eye,JITTER,0.0)
            else:
                gid=lax.broadcasted_iota(jnp.int32,(B,B),1)+(off_ref[0]+(j-nb)*B)
                k=k+jnp.where(gid==lax.broadcasted_iota(jnp.int32,(B,B),0)+i*B,JITTER,0.0)
            a_ref[i,j]=k

def body(off_ref,panel_ref,own_ref,chol_ref,prec_ref,a_ref,u_ref,l_ref,r_ref,w_ref,uk_ref,m_ref,*,own):
    nb=panel_ref.shape[0]//B; no=own//B; nj=nb+no
    eye=lax.broadcasted_iota(jnp.int32,(B,B),0)==lax.broadcasted_iota(jnp.int32,(B,B),1)
    kern_init(off_ref,panel_ref,own_ref,a_ref,nb,no)
    r_ref[...]=a_ref[0,0]
    u_ref[...]=jnp.zeros_like(u_ref); l_ref[...]=jnp.zeros_like(l_ref)
    def step(s,carry):
        ph=s//nb; K=s-ph*nb
        factor128(r_ref,w_ref,uk_ref,m_ref)
        lrow=jnp.concatenate([l_ref[K,t] for t in range(nb)],axis=1)
        M=m_ref[...]
        ua=u_ref[...]
        upd=mmul(lrow,ua)
        ar=jnp.concatenate([a_ref[K,j] for j in range(nj)],axis=1)-upd
        un=mmul(M,ar)
        for j in range(nj):
            v=un[:,j*B:(j+1)*B]
            if j<nb:
                v=jnp.where(j>K,v,0.0); v=jnp.where(j==K,uk_ref[...],v)
            u_ref[pl.ds(pl.multiple_of(K*B,B),B),j*B:(j+1)*B]=v
            l_ref[j,K]=v.T
        K1=jnp.minimum(K+1,nb-1)
        @pl.when(K<nb-1)
        def _():
            z=a_ref[K1,K1]
            lr=jnp.concatenate([l_ref[K1,t] for t in range(nb)],axis=1)
            r_ref[...]=z-mmul_nt(lr,lr)
        @pl.when(s==nb-1)
        def _():
            for i in range(no):
                for t in range(nb):
                    chol_ref[i*B:(i+1)*B,t*B:(t+1)*B]=l_ref[nb+i,t]
            for J in range(nb):
                for C in range(J,nb):
                    x=u_ref[J*B:(J+1)*B,C*B:nb*B]; y=u_ref[C*B:(C+1)*B,C*B:nb*B]
                    acc=mmul_nt(x,y)
                    if J==C: acc=acc+jnp.where(eye,SHIFT,0.0)
                    a_ref[J,C]=acc
            r_ref[...]=a_ref[0,0]
            u_ref[...]=jnp.zeros_like(u_ref); l_ref[...]=jnp.zeros_like(l_ref)
        return carry
    lax.fori_loop(0,2*nb,step,0)
    for J in range(nb):
        for C in range(nb):
            prec_ref[J*B:(J+1)*B,C*B:(C+1)*B]=l_ref[J,C]

def chol_kernel(off,panel,own):
    n=panel.shape[0]; ro=own.shape[0]; nb=n//B; no=ro//B
    vm=pl.BlockSpec(memory_space=pltpu.VMEM)
    f32=jnp.float32
    return pl.pallas_call(functools.partial(body,own=ro),
        out_shape=(jax.ShapeDtypeStruct((ro,n),f32),jax.ShapeDtypeStruct((n,n),f32)),
        in_specs=[pl.BlockSpec(memory_space=pltpu.SMEM),vm,vm],out_specs=(vm,vm),
        scratch_shapes=[pltpu.VMEM((nb,nb+no,B,B),f32),pltpu.VMEM((n,n+ro),f32),pltpu.VMEM((nb+no,nb,B,B),f32)]+[pltpu.VMEM((B,B),f32)]*4,
        name='chol')(off,panel,own)


from jax.sharding import PartitionSpec as P

PANEL = 512
GRAM_SCALE = 64.0


def swap(x, axis, d):
    n = lax.axis_size(axis)
    return lax.ppermute(x, axis, [(i, i ^ d) for i in range(n)])


def panel_everywhere(panel):
    ctrs = lax.axis_size("ctr")
    samps = lax.axis_size("samp")
    me = lax.axis_index("samp")
    rows = panel.shape[0] // samps
    chunk = lax.dynamic_slice_in_dim(panel, me * rows, rows, 0)
    got = [lax.ppermute(chunk, "ctr", [(0, d)]) for d in range(1, ctrs)]
    total = got[0]
    for piece in got[1:]:
        total = total + piece
    chunk = jnp.where(lax.axis_index("ctr") == 0, chunk, total)
    parts = jnp.stack([chunk] + [swap(chunk, "samp", d) for d in range(1, samps)])
    return jnp.take(parts, jnp.arange(samps) ^ me, axis=0).reshape(panel.shape)


def sample_scatter(part):
    samps = lax.axis_size("samp")
    me = lax.axis_index("samp")
    rows = part.shape[0] // samps
    blocks = part.reshape(samps // 2, 2, rows, part.shape[1])
    side = me & 1
    mine = lax.dynamic_index_in_dim(blocks, side, 1, False)
    other = lax.dynamic_index_in_dim(blocks, 1 - side, 1, False)
    half = mine + swap(other, "samp", 1)
    k = me >> 1
    total = lax.dynamic_index_in_dim(half, k, 0, False)
    for d in range(1, samps // 2):
        total = total + swap(lax.dynamic_index_in_dim(half, k ^ d, 0, False), "samp", 2 * d)
    return total


def kernel_block(first_set, second_set):
    cross_dot = lax.dot_general(
        first_set, second_set, (((1,), (1,)), ((), ())), preferred_element_type=jnp.float32
    )
    first_sq = jnp.sum(jnp.square(first_set.astype(jnp.float32)), axis=1)
    second_sq = jnp.sum(jnp.square(second_set.astype(jnp.float32)), axis=1)
    sq_dist = jnp.maximum(first_sq[:, None] + second_sq[None, :] - 2.0 * cross_dot, 0.0)
    return jnp.exp(-(2.0 / first_set.shape[1]) * sq_dist)


def local(samples, centers):
    samp_count = lax.axis_size("samp")
    samp_index = lax.axis_index("samp")
    ctr_index = lax.axis_index("ctr")
    mc_dev = centers.shape[0]
    row_dev = mc_dev // samp_count
    panel = panel_everywhere(centers[:PANEL])
    kern_own = kernel_block(centers, samples).astype(jnp.bfloat16)
    kern_panel = kernel_block(samples, panel).astype(jnp.bfloat16)
    part = jnp.dot(kern_own, kern_panel, preferred_element_type=jnp.float32)
    gram = sample_scatter(part) * (GRAM_SCALE / (samples.shape[0] * samp_count))
    own = lax.dynamic_slice_in_dim(centers, samp_index * row_dev, row_dev, 0)
    pad = -row_dev % B
    own = jnp.pad(own, ((0, pad), (0, 0)))
    off = (ctr_index * mc_dev + samp_index * row_dev).astype(jnp.int32).reshape(1)
    chol, precond = chol_kernel(off, panel, own)
    return (gram[None], chol[None, :row_dev], precond)


def solution(mesh):
    placed = (P("samp", None), P("ctr", None))
    return jax.shard_map(
        local,
        mesh=mesh,
        in_specs=placed,
        out_specs=(P("ctr", "samp", None), P("ctr", "samp", None), P()),
        check_vma=False,
    )
```

```python
import functools
import jax, jax.numpy as jnp
from jax import lax
from jax.experimental import pallas as pl
from jax.experimental.pallas import tpu as pltpu
JITTER=0.01; SHIFT=0.5
RATIO=1.0/64
B=128
VB=32
HI=lax.Precision.HIGHEST
def mmul(a,b): return jnp.dot(a,b,preferred_element_type=jnp.float32,precision=HI)
def mmul_nt(a,b): return lax.dot_general(a,b,(((1,),(1,)),((),())),preferred_element_type=jnp.float32,precision=HI)
def lanebc(x,c): return jnp.broadcast_to(x[:,c:c+1],(8,B))
def subbc(x,j): return jnp.broadcast_to(x[j:j+1,:],(8,B))

def factor128(probs):
    row=lax.broadcasted_iota(jnp.int32,(B,B),0)
    lane=lax.broadcasted_iota(jnp.int32,(B,B),1)
    n=VB//8
    for r,w,u,m in probs: w[...]=jnp.where(lane==row,1.0,0.0)
    for b in range(B//VB):
        base=b*VB
        st=[]
        for r,w,u,m in probs:
            st.append(([r[base+8*k:base+8*k+8,:] for k in range(n)],[w[base+8*k:base+8*k+8,:] for k in range(n)]))
        for i in range(n):
            loc=[]
            for X,Y in st:
                g=[lanebc(X[i],base+8*i+j) for j in range(8)]
                c={k:[lanebc(X[k],base+8*i+j) for j in range(8)] for k in range(i+1,n)}
                loc.append([g,c,X[i],Y[i]])
            for j in range(8):
                k=base+8*i+j
                for (r,w,u,m),(X,Y),L in zip(probs,st,loc):
                    g,c,a,y=L
                    rs=lax.rsqrt(subbc(g[j],j))
                    q=[None]*8
                    lj=g[j]*rs
                    for t in range(j+1,8):
                        q[t]=subbc(g[t],j)*rs
                        g[t]=g[t]-lj*q[t]
                    ur=subbc(a,j)*rs; wr=subbc(y,j)*rs
                    if j<7:
                        L[2]=a-lj*ur; L[3]=y-lj*wr
                    u[k:k+1,:]=ur[0:1]; m[k:k+1,:]=wr[0:1]
                    for z in range(i+1,n):
                        cj=c[z][j]*rs
                        for t in range(j+1,8): c[z][t]=c[z][t]-cj*q[t]
                        X[z]=X[z]-cj*ur; Y[z]=Y[z]-cj*wr
        e=base+VB
        if e<B:
            for r,w,u,m in probs:
                ub=u[base:e,:]; mb=m[base:e,:]
                z=mmul(ub.T[e:,:],jnp.concatenate([ub,mb],axis=1))
                r[e:,:]=r[e:,:]-z[:,:B]
                w[e:,:]=w[e:,:]-z[:,B:]
    for r,w,u,m in probs: u[...]=jnp.where(lane>=row,u[...],0.0)

def kern_init(off_ref,panel_ref,own_ref,a_ref,nb,no):
    pan=panel_ref[...]; ow=own_ref[...]
    def bdot(a,b): return lax.dot_general(a,b,(((1,),(1,)),((),())),preferred_element_type=jnp.float32)
    c=-(2.0/panel_ref.shape[1])
    eye=lax.broadcasted_iota(jnp.int32,(B,B),0)==lax.broadcasted_iota(jnp.int32,(B,B),1)
    def diagrow(x):
        d=jnp.where(eye,x,0.0)
        return jnp.sum(d,axis=0,keepdims=True), jnp.sum(d,axis=1,keepdims=True)
    rows=[];cols=[]
    for i in range(nb):
        pi=pan[i*B:(i+1)*B]
        r,cc=diagrow(bdot(pi,pi)); rows.append(r); cols.append(cc)
    for i in range(no):
        oi=ow[i*B:(i+1)*B]
        r,_=diagrow(bdot(oi,oi)); rows.append(r)
    for i in range(nb):
        for j in range(nb+no):
            rhs=pan[j*B:(j+1)*B] if j<nb else ow[(j-nb)*B:(j-nb+1)*B]
            x=bdot(pan[i*B:(i+1)*B],rhs)
            k=jnp.exp(c*jnp.maximum(cols[i]+rows[j]-2.0*x,0.0))
            if j<nb:
                if i==j: k=k+jnp.where(eye,JITTER,0.0)
            else:
                gid=lax.broadcasted_iota(jnp.int32,(B,B),1)+(off_ref[0]+(j-nb)*B)
                k=k+jnp.where(gid==lax.broadcasted_iota(jnp.int32,(B,B),0)+i*B,JITTER,0.0)
            a_ref[i,j]=k

def put(M,uk,row,K,nb,u_ref,l_ref):
    un=mmul(M,jnp.concatenate(row,axis=1))
    for j in range(len(row)):
        v=un[:,j*B:(j+1)*B]
        if j<nb:
            v=jnp.where(j>K,v,0.0); v=jnp.where(j==K,uk,v)
        u_ref[K,j]=v
        l_ref[j,K]=v.T

def trail(a_ref,u_ref,l_ref,Kp,nb,nj):
    for i in range(1,nb):
        z=mmul(l_ref[i,Kp],jnp.concatenate([u_ref[Kp,j] for j in range(i,nj)],axis=1))
        for j in range(i,nj):
            a_ref[i,j]=a_ref[i,j]-z[:,(j-i)*B:(j-i+1)*B]

def body(off_ref,panel_ref,own_ref,chol_ref,prec_ref,a_ref,u_ref,l_ref,s_ref,v_ref,h_ref,ms_ref,r0,w0,k0,m0,r1,w1,k1,m1,*,own):
    nb=panel_ref.shape[0]//B; no=own//B; nj=nb+no
    eye=lax.broadcasted_iota(jnp.int32,(B,B),0)==lax.broadcasted_iota(jnp.int32,(B,B),1)
    kern_init(off_ref,panel_ref,own_ref,a_ref,nb,no)
    zero=jnp.zeros((B,B),jnp.float32)
    for j in range(nj):
        u_ref[nb,j]=zero; l_ref[j,nb]=zero
    for j in range(nb):
        v_ref[nb,j]=zero; h_ref[j,nb]=zero
    kr=[jnp.concatenate([a_ref[i,j] for j in range(nb)],axis=1) for i in range(nb)]
    kc=jnp.concatenate(kr,axis=0)
    top=None
    for i in range(nb):
        z=mmul(kr[i],kc[:,i*B:])+SHIFT*kr[i][:,i*B:]
        for j in range(i,nb):
            s_ref[i,j]=z[:,(j-i)*B:(j-i+1)*B]
        d=jnp.where(eye,s_ref[i,i],0.0)
        top=d if top is None else jnp.maximum(top,d)
    r0[...]=a_ref[0,0]; r1[...]=s_ref[0,0]
    def step(K,low):
        Kp=jnp.where(K==0,nb,K-1)
        factor128([(r0,w0,k0,m0),(r1,w1,k1,m1)])
        trail(a_ref,u_ref,l_ref,Kp,nb,nj)
        trail(s_ref,v_ref,h_ref,Kp,nb,nb)
        ms_ref[K]=m0[...]
        put(m0[...],k0[...],[a_ref[K,j] for j in range(nj)],K,nb,u_ref,l_ref)
        put(m1[...],k1[...],[s_ref[K,j] for j in range(nb)],K,nb,v_ref,h_ref)
        K1=jnp.minimum(K+1,nb-1)
        r0[...]=a_ref[K1,K1]-mmul(l_ref[K1,K],u_ref[K,K1])
        r1[...]=s_ref[K1,K1]-mmul(h_ref[K1,K],v_ref[K,K1])
        x=k1[...]
        return jnp.minimum(low,jnp.where(eye,x*x,1e30))
    low=lax.fori_loop(0,nb,step,jnp.full((B,B),1e30,jnp.float32))
    for i in range(no):
        for t in range(nb):
            chol_ref[i*B:(i+1)*B,t*B:(t+1)*B]=l_ref[nb+i,t]
    good=jnp.min(low)>=RATIO*jnp.max(top)
    @pl.when(good)
    def _():
        g=[]
        for K in range(nb):
            c=jnp.concatenate([h_ref[K,J] for J in range(K+1)],axis=1)
            for t in range(K):
                z=mmul(l_ref[K,t],g[t])
                c=jnp.concatenate([c[:,:(t+1)*B]-z,c[:,(t+1)*B:]],axis=1)
            g.append(mmul(ms_ref[K],c))
        for K in range(nb):
            for J in range(nb):
                prec_ref[K*B:(K+1)*B,J*B:(J+1)*B]=g[K][:,J*B:(J+1)*B] if J<=K else zero
    @pl.when(jnp.logical_not(good))
    def _():
        for C in range(nb):
            rows=[jnp.concatenate([u_ref[J,I] for I in range(C,nb)],axis=1) for J in range(C+1)]
            acc=mmul_nt(jnp.concatenate(rows,axis=0),rows[C])
            for J in range(C+1):
                v=acc[J*B:(J+1)*B]
                if J==C: v=v+jnp.where(eye,SHIFT,0.0)
                s_ref[J,C]=v
        for j in range(nb):
            v_ref[nb,j]=zero; h_ref[j,nb]=zero
        r1[...]=s_ref[0,0]
        def again(K,carry):
            Kp=jnp.where(K==0,nb,K-1)
            factor128([(r1,w1,k1,m1)])
            trail(s_ref,v_ref,h_ref,Kp,nb,nb)
            put(m1[...],k1[...],[s_ref[K,j] for j in range(nb)],K,nb,v_ref,h_ref)
            K1=jnp.minimum(K+1,nb-1)
            r1[...]=s_ref[K1,K1]-mmul(h_ref[K1,K],v_ref[K,K1])
            return carry
        lax.fori_loop(0,nb,again,0)
        for J in range(nb):
            for C in range(nb):
                prec_ref[J*B:(J+1)*B,C*B:(C+1)*B]=h_ref[J,C]

def chol_kernel(off,panel,own):
    n=panel.shape[0]; ro=own.shape[0]; nb=n//B; no=ro//B; nj=nb+no
    vm=pl.BlockSpec(memory_space=pltpu.VMEM)
    f32=jnp.float32
    V=lambda *s: pltpu.VMEM(s+(B,B),f32)
    return pl.pallas_call(functools.partial(body,own=ro),
        out_shape=(jax.ShapeDtypeStruct((ro,n),f32),jax.ShapeDtypeStruct((n,n),f32)),
        in_specs=[pl.BlockSpec(memory_space=pltpu.SMEM),vm,vm],out_specs=(vm,vm),
        scratch_shapes=[V(nb,nj),V(nb+1,nj),V(nj,nb+1),V(nb,nb),V(nb+1,nb),V(nb,nb+1),V(nb)]+[V()]*8,
        name='chol')(off,panel,own)


LOG2E = 1.4426950408889634


def row_norms(x, scale):
    sq = jnp.square(x.astype(jnp.float32))
    hi = sq.astype(jnp.bfloat16)
    lo = (sq - hi.astype(jnp.float32)).astype(jnp.bfloat16)
    one = jnp.ones((8, x.shape[1]), jnp.bfloat16)
    dims = (((1,), (1,)), ((), ()))
    out = lax.dot_general(one, hi, dims, preferred_element_type=jnp.float32)
    out = out + lax.dot_general(one, lo, dims, preferred_element_type=jnp.float32)
    return out[0:1] * scale


def col_norms(x, scale):
    return jnp.sum(jnp.square(x.astype(jnp.float32)), axis=1, keepdims=True) * scale


def kern_tile(x, y, xcol, yrow):
    dot = lax.dot_general(x, y, (((1,), (1,)), ((), ())), preferred_element_type=jnp.float32)
    arg = jnp.minimum(dot * (4.0 * LOG2E / x.shape[1]) + (xcol + yrow), 0.0)
    return jnp.exp2(arg).astype(jnp.bfloat16)


def own_body(c_ref, s_ref, o_ref):
    scale = -2.0 * LOG2E / c_ref.shape[1]
    s = s_ref[...]
    yrow = row_norms(s, scale)
    for r in range(c_ref.shape[0] // B):
        c = c_ref[r * B : (r + 1) * B, :]
        o_ref[r * B : (r + 1) * B, :] = kern_tile(c, s, col_norms(c, scale), yrow)


def own_kernel(centers, samples, tile=512):
    mc, d = centers.shape
    ns = samples.shape[0]
    return pl.pallas_call(
        own_body,
        grid=(ns // tile,),
        in_specs=[pl.BlockSpec((mc, d), lambda t: (0, 0)), pl.BlockSpec((tile, d), lambda t: (t, 0))],
        out_specs=pl.BlockSpec((mc, tile), lambda t: (0, t)),
        out_shape=jax.ShapeDtypeStruct((mc, ns), jnp.bfloat16),
        name="kern_own",
    )(centers, samples)


def gram_body(me_ref, *refs, tiles):
    pieces, (k_ref, s_ref, other_ref, mine_ref, panel_ref, acc_ref, row_ref) = refs[:-7], refs[-7:]
    samps = len(pieces)
    t = pl.program_id(0)
    me = me_ref[0]
    scale = -2.0 * LOG2E / s_ref.shape[1]

    @pl.when(t == 0)
    def _():
        rows = pieces[0].shape[0]
        for d in range(samps):
            at = pl.multiple_of((me ^ d) * rows, rows)
            panel_ref[pl.ds(at, rows), :] = pieces[d][...]
        row_ref[...] = row_norms(panel_ref[...], scale)
        acc_ref[...] = jnp.zeros_like(acc_ref)

    panel = panel_ref[...]
    yrow = row_ref[...]
    kp = []
    for r in range(s_ref.shape[0] // B):
        s = s_ref[r * B : (r + 1) * B, :]
        kp.append(kern_tile(s, panel, col_norms(s, scale), yrow))
    acc_ref[...] += jnp.dot(k_ref[...], jnp.concatenate(kp, axis=0), preferred_element_type=jnp.float32)

    @pl.when(t == tiles - 1)
    def _():
        side = me & 1
        k = me >> 1
        rows = other_ref.shape[1]
        for d in range(samps // 2):
            at = (k ^ d) * 2
            mine_ref[d] = acc_ref[pl.ds(pl.multiple_of((at + side) * rows, rows), rows), :]
            other_ref[d] = acc_ref[pl.ds(pl.multiple_of((at + 1 - side) * rows, rows), rows), :]


def gram_kernel(me, pieces, kern_own, samples, tile=512):
    samps = len(pieces)
    mc, ns = kern_own.shape
    d = samples.shape[1]
    width = samps * pieces[0].shape[0]
    rows = mc // samps
    inside = pl.BlockSpec(memory_space=pltpu.VMEM)
    half = jax.ShapeDtypeStruct((samps // 2, rows, width), jnp.float32)
    return pl.pallas_call(
        functools.partial(gram_body, tiles=ns // tile),
        grid=(ns // tile,),
        in_specs=[pl.BlockSpec(memory_space=pltpu.SMEM)]
        + [inside] * samps
        + [pl.BlockSpec((mc, tile), lambda t: (0, t)), pl.BlockSpec((tile, d), lambda t: (t, 0))],
        out_specs=(inside, inside, inside),
        out_shape=(half, half, jax.ShapeDtypeStruct((width, d), jnp.bfloat16)),
        scratch_shapes=[pltpu.VMEM((mc, width), jnp.float32), pltpu.VMEM((1, width), jnp.float32)],
        name="gram",
    )(me, *pieces, kern_own, samples)


from jax.sharding import PartitionSpec as P

PANEL = 512
GRAM_SCALE = 64.0


def swap(x, axis, d):
    n = lax.axis_size(axis)
    return lax.ppermute(x, axis, [(i, i ^ d) for i in range(n)])


def panel_pieces(centers):
    ctrs = lax.axis_size("ctr")
    samps = lax.axis_size("samp")
    rows = PANEL // samps
    chunk = lax.dynamic_slice_in_dim(centers, lax.axis_index("samp") * rows, rows, 0)
    got = [lax.ppermute(chunk, "ctr", [(0, d)]) for d in range(1, ctrs)]
    total = got[0]
    for piece in got[1:]:
        total = total + piece
    chunk = jnp.where(lax.axis_index("ctr") == 0, chunk, total)
    return [chunk] + [swap(chunk, "samp", d) for d in range(1, samps)]


def local(samples, centers):
    samp_count = lax.axis_size("samp")
    samp_index = lax.axis_index("samp").astype(jnp.int32)
    ctr_index = lax.axis_index("ctr").astype(jnp.int32)
    mc_dev = centers.shape[0]
    row_dev = mc_dev // samp_count
    own = lax.dynamic_slice_in_dim(centers, samp_index * row_dev, row_dev, 0)
    own = jnp.pad(own, ((0, -row_dev % B), (0, 0)))
    pieces = panel_pieces(centers)
    kern_own = own_kernel(centers, samples)
    other, mine, panel = gram_kernel(samp_index.reshape(1), pieces, kern_own, samples)
    half = mine + swap(other, "samp", 1)
    total = half[0]
    for d in range(1, samp_count // 2):
        total = total + swap(half[d], "samp", 2 * d)
    gram = total * (GRAM_SCALE / (samples.shape[0] * samp_count))
    off = (ctr_index * mc_dev + samp_index * row_dev).reshape(1)
    chol, precond = chol_kernel(off, panel, own)
    return (gram[None], chol[None, :row_dev], precond)


def solution(mesh):
    placed = (P("samp", None), P("ctr", None))
    return jax.shard_map(
        local,
        mesh=mesh,
        in_specs=placed,
        out_specs=(P("ctr", "samp", None), P("ctr", "samp", None), P()),
        check_vma=False,
    )
```

```python
import functools
import jax, jax.numpy as jnp
from jax import lax
from jax.experimental import pallas as pl
from jax.experimental.pallas import tpu as pltpu
JITTER=0.01; SHIFT=0.5
RATIO=1.0/64
B=128
VB=32
HI=lax.Precision.HIGHEST
def mmul(a,b): return jnp.dot(a,b,preferred_element_type=jnp.float32,precision=HI)
def mmul_nt(a,b): return lax.dot_general(a,b,(((1,),(1,)),((),())),preferred_element_type=jnp.float32,precision=HI)
def lanebc(x,c): return jnp.broadcast_to(x[:,c:c+1],(8,B))
def subbc(x,j): return jnp.broadcast_to(x[j:j+1,:],(8,B))

def factor128(probs):
    row=lax.broadcasted_iota(jnp.int32,(B,B),0)
    lane=lax.broadcasted_iota(jnp.int32,(B,B),1)
    n=VB//8
    for r,w,u,m in probs: w[...]=jnp.where(lane==row,1.0,0.0)
    for b in range(B//VB):
        base=b*VB
        st=[]
        for r,w,u,m in probs:
            st.append(([r[base+8*k:base+8*k+8,:] for k in range(n)],[w[base+8*k:base+8*k+8,:] for k in range(n)]))
        for i in range(n):
            loc=[]
            for X,Y in st:
                g=[lanebc(X[i],base+8*i+j) for j in range(8)]
                c={k:[lanebc(X[k],base+8*i+j) for j in range(8)] for k in range(i+1,n)}
                loc.append([g,c,X[i],Y[i]])
            for j in range(8):
                k=base+8*i+j
                for (r,w,u,m),(X,Y),L in zip(probs,st,loc):
                    g,c,a,y=L
                    rs=lax.rsqrt(subbc(g[j],j))
                    q=[None]*8
                    lj=g[j]*rs
                    for t in range(j+1,8):
                        q[t]=subbc(g[t],j)*rs
                        g[t]=g[t]-lj*q[t]
                    ur=subbc(a,j)*rs; wr=subbc(y,j)*rs
                    if j<7:
                        L[2]=a-lj*ur; L[3]=y-lj*wr
                    u[k:k+1,:]=ur[0:1]; m[k:k+1,:]=wr[0:1]
                    for z in range(i+1,n):
                        cj=c[z][j]*rs
                        for t in range(j+1,8): c[z][t]=c[z][t]-cj*q[t]
                        X[z]=X[z]-cj*ur; Y[z]=Y[z]-cj*wr
        e=base+VB
        if e<B:
            for r,w,u,m in probs:
                ub=u[base:e,:]; mb=m[base:e,:]
                z=mmul(ub.T[e:,:],jnp.concatenate([ub,mb],axis=1))
                r[e:,:]=r[e:,:]-z[:,:B]
                w[e:,:]=w[e:,:]-z[:,B:]
    for r,w,u,m in probs: u[...]=jnp.where(lane>=row,u[...],0.0)

def kern_init(off_ref,panel_ref,own_ref,a_ref,nb,no):
    pan=panel_ref[...]; ow=own_ref[...]
    def bdot(a,b): return lax.dot_general(a,b,(((1,),(1,)),((),())),preferred_element_type=jnp.float32)
    c=-(2.0/panel_ref.shape[1])
    eye=lax.broadcasted_iota(jnp.int32,(B,B),0)==lax.broadcasted_iota(jnp.int32,(B,B),1)
    def diagrow(x):
        d=jnp.where(eye,x,0.0)
        return jnp.sum(d,axis=0,keepdims=True), jnp.sum(d,axis=1,keepdims=True)
    rows=[];cols=[]
    for i in range(nb):
        pi=pan[i*B:(i+1)*B]
        r,cc=diagrow(bdot(pi,pi)); rows.append(r); cols.append(cc)
    for i in range(no):
        oi=ow[i*B:(i+1)*B]
        r,_=diagrow(bdot(oi,oi)); rows.append(r)
    for i in range(nb):
        for j in range(nb+no):
            rhs=pan[j*B:(j+1)*B] if j<nb else ow[(j-nb)*B:(j-nb+1)*B]
            x=bdot(pan[i*B:(i+1)*B],rhs)
            k=jnp.exp(c*jnp.maximum(cols[i]+rows[j]-2.0*x,0.0))
            if j<nb:
                if i==j: k=k+jnp.where(eye,JITTER,0.0)
            else:
                gid=lax.broadcasted_iota(jnp.int32,(B,B),1)+(off_ref[0]+(j-nb)*B)
                k=k+jnp.where(gid==lax.broadcasted_iota(jnp.int32,(B,B),0)+i*B,JITTER,0.0)
            a_ref[i,j]=k

def put(M,uk,row,K,nb,u_ref,l_ref):
    un=mmul(M,jnp.concatenate(row,axis=1))
    for j in range(len(row)):
        v=un[:,j*B:(j+1)*B]
        if j<nb:
            v=jnp.where(j>K,v,0.0); v=jnp.where(j==K,uk,v)
        u_ref[K,j]=v
        l_ref[j,K]=v.T

def trail(a_ref,u_ref,l_ref,Kp,nb,nj):
    for i in range(1,nb):
        z=mmul(l_ref[i,Kp],jnp.concatenate([u_ref[Kp,j] for j in range(i,nj)],axis=1))
        for j in range(i,nj):
            a_ref[i,j]=a_ref[i,j]-z[:,(j-i)*B:(j-i+1)*B]

def body(off_ref,panel_ref,own_ref,chol_ref,prec_ref,a_ref,u_ref,l_ref,s_ref,v_ref,h_ref,ms_ref,r0,w0,k0,m0,r1,w1,k1,m1,*,own):
    nb=panel_ref.shape[0]//B; no=own//B; nj=nb+no
    eye=lax.broadcasted_iota(jnp.int32,(B,B),0)==lax.broadcasted_iota(jnp.int32,(B,B),1)
    kern_init(off_ref,panel_ref,own_ref,a_ref,nb,no)
    zero=jnp.zeros((B,B),jnp.float32)
    for j in range(nj):
        u_ref[nb,j]=zero; l_ref[j,nb]=zero
    for j in range(nb):
        v_ref[nb,j]=zero; h_ref[j,nb]=zero
    kr=[jnp.concatenate([a_ref[i,j] for j in range(nb)],axis=1) for i in range(nb)]
    kc=jnp.concatenate(kr,axis=0)
    top=None
    for i in range(nb):
        z=mmul(kr[i],kc[:,i*B:])+SHIFT*kr[i][:,i*B:]
        for j in range(i,nb):
            s_ref[i,j]=z[:,(j-i)*B:(j-i+1)*B]
        d=jnp.where(eye,s_ref[i,i],0.0)
        top=d if top is None else jnp.maximum(top,d)
    r0[...]=a_ref[0,0]; r1[...]=s_ref[0,0]
    def step(K,low):
        Kp=jnp.where(K==0,nb,K-1)
        factor128([(r0,w0,k0,m0),(r1,w1,k1,m1)])
        trail(a_ref,u_ref,l_ref,Kp,nb,nj)
        trail(s_ref,v_ref,h_ref,Kp,nb,nb)
        ms_ref[K]=m0[...]
        put(m0[...],k0[...],[a_ref[K,j] for j in range(nj)],K,nb,u_ref,l_ref)
        put(m1[...],k1[...],[s_ref[K,j] for j in range(nb)],K,nb,v_ref,h_ref)
        K1=jnp.minimum(K+1,nb-1)
        r0[...]=a_ref[K1,K1]-mmul(l_ref[K1,K],u_ref[K,K1])
        r1[...]=s_ref[K1,K1]-mmul(h_ref[K1,K],v_ref[K,K1])
        x=k1[...]
        return jnp.minimum(low,jnp.where(eye,x*x,1e30))
    low=lax.fori_loop(0,nb,step,jnp.full((B,B),1e30,jnp.float32))
    for i in range(no):
        for t in range(nb):
            chol_ref[i*B:(i+1)*B,t*B:(t+1)*B]=l_ref[nb+i,t]
    good=jnp.min(low)>=RATIO*jnp.max(top)
    @pl.when(good)
    def _():
        g=[]
        for K in range(nb):
            c=jnp.concatenate([h_ref[K,J] for J in range(K+1)],axis=1)
            for t in range(K):
                z=mmul(l_ref[K,t],g[t])
                c=jnp.concatenate([c[:,:(t+1)*B]-z,c[:,(t+1)*B:]],axis=1)
            g.append(mmul(ms_ref[K],c))
        for K in range(nb):
            for J in range(nb):
                prec_ref[K*B:(K+1)*B,J*B:(J+1)*B]=g[K][:,J*B:(J+1)*B] if J<=K else zero
    @pl.when(jnp.logical_not(good))
    def _():
        for C in range(nb):
            rows=[jnp.concatenate([u_ref[J,I] for I in range(C,nb)],axis=1) for J in range(C+1)]
            acc=mmul_nt(jnp.concatenate(rows,axis=0),rows[C])
            for J in range(C+1):
                v=acc[J*B:(J+1)*B]
                if J==C: v=v+jnp.where(eye,SHIFT,0.0)
                s_ref[J,C]=v
        for j in range(nb):
            v_ref[nb,j]=zero; h_ref[j,nb]=zero
        r1[...]=s_ref[0,0]
        def again(K,carry):
            Kp=jnp.where(K==0,nb,K-1)
            factor128([(r1,w1,k1,m1)])
            trail(s_ref,v_ref,h_ref,Kp,nb,nb)
            put(m1[...],k1[...],[s_ref[K,j] for j in range(nb)],K,nb,v_ref,h_ref)
            K1=jnp.minimum(K+1,nb-1)
            r1[...]=s_ref[K1,K1]-mmul(h_ref[K1,K],v_ref[K,K1])
            return carry
        lax.fori_loop(0,nb,again,0)
        for J in range(nb):
            for C in range(nb):
                prec_ref[J*B:(J+1)*B,C*B:(C+1)*B]=h_ref[J,C]

def chol_kernel(off,panel,own):
    n=panel.shape[0]; ro=own.shape[0]; nb=n//B; no=ro//B; nj=nb+no
    vm=pl.BlockSpec(memory_space=pltpu.VMEM)
    f32=jnp.float32
    V=lambda *s: pltpu.VMEM(s+(B,B),f32)
    return pl.pallas_call(functools.partial(body,own=ro),
        out_shape=(jax.ShapeDtypeStruct((ro,n),f32),jax.ShapeDtypeStruct((n,n),f32)),
        in_specs=[pl.BlockSpec(memory_space=pltpu.SMEM),vm,vm],out_specs=(vm,vm),
        scratch_shapes=[V(nb,nj),V(nb+1,nj),V(nj,nb+1),V(nb,nb),V(nb+1,nb),V(nb,nb+1),V(nb)]+[V()]*8,
        compiler_params=pltpu.CompilerParams(vmem_limit_bytes=24<<20),
        name='chol')(off,panel,own)


LOG2E = 1.4426950408889634


def near(x):
    return pltpu.with_memory_space_constraint(x, pltpu.VMEM)


def square_parts(x):
    sq = jnp.square(x.astype(jnp.float32))
    hi = sq.astype(jnp.bfloat16)
    return hi, (sq - hi.astype(jnp.float32)).astype(jnp.bfloat16)


def nt(a, b):
    return lax.dot_general(a, b, (((1,), (1,)), ((), ())), preferred_element_type=jnp.float32)


def row_norms(x, scale):
    hi, lo = square_parts(x)
    one = jnp.ones((8, x.shape[1]), jnp.bfloat16)
    return (nt(one, hi) + nt(one, lo))[0:1] * scale


def col_norms(x, scale):
    hi, lo = square_parts(x)
    one = jnp.ones((x.shape[1], B), jnp.bfloat16)
    dot = lambda a: jnp.dot(a, one, preferred_element_type=jnp.float32)
    return (dot(hi) + dot(lo)) * scale


def kern_tile(x, y, xcol, yrow):
    dot = nt(x, y)
    both = jnp.concatenate([xcol] * (y.shape[0] // B), axis=1) + yrow
    arg = jnp.minimum(dot * (4.0 * LOG2E / x.shape[1]) + both, 0.0)
    return jnp.exp2(arg).astype(jnp.bfloat16)


def own_body(me_ref, c_ref, s_ref, k_ref, norm_ref, own_ref, *, row_dev):
    scale = -2.0 * LOG2E / c_ref.shape[1]
    at = pl.multiple_of(me_ref[0] * row_dev, row_dev)
    own_ref[0:row_dev, :] = c_ref[pl.ds(at, row_dev), :]
    if row_dev < own_ref.shape[0]:
        own_ref[row_dev:, :] = jnp.zeros((own_ref.shape[0] - row_dev, own_ref.shape[1]), own_ref.dtype)
    c = c_ref[...]
    ccol = col_norms(c, scale)
    tile = 2 * B
    for t in range(0, s_ref.shape[0], tile):
        s = s_ref[t : t + tile, :]
        norm_ref[t : t + tile, :] = col_norms(s, scale)
        k_ref[:, t : t + tile] = kern_tile(c, s, ccol, row_norms(s, scale))


def own_kernel(me, centers, samples, row_dev):
    mc, d = centers.shape
    ns = samples.shape[0]
    inside = pl.BlockSpec(memory_space=pltpu.VMEM)
    return pl.pallas_call(
        functools.partial(own_body, row_dev=row_dev),
        in_specs=[pl.BlockSpec(memory_space=pltpu.SMEM), inside, inside],
        out_specs=(inside, inside, inside),
        out_shape=(
            pltpu.VMEM((mc, ns), jnp.bfloat16),
            pltpu.VMEM((ns, B), jnp.float32),
            pltpu.VMEM((row_dev + -row_dev % B, d), jnp.bfloat16),
        ),
        compiler_params=pltpu.CompilerParams(vmem_limit_bytes=16 << 20),
        name="kern_own",
    )(me, near(centers), samples)


def gram_body(me_ref, *refs, samps, tile):
    pieces, (k_ref, s_ref, norm_ref) = refs[:samps], refs[samps : samps + 3]
    panel_ref, other_ref = refs[samps + 3 : samps + 5]
    mine, (acc_ref, kp_ref) = refs[samps + 5 : -2], refs[-2:]
    me = me_ref[0]
    rows = pieces[0].shape[0]
    for d in range(samps):
        panel_ref[pl.ds(pl.multiple_of((me ^ d) * rows, rows), rows), :] = pieces[d][...]
    panel = panel_ref[...]
    yrow = row_norms(panel, -2.0 * LOG2E / s_ref.shape[1])
    for t in range(0, s_ref.shape[0], tile):
        kp_ref[t : t + tile, :] = kern_tile(s_ref[t : t + tile, :], panel, norm_ref[t : t + tile, :], yrow)
    acc_ref[...] = jnp.dot(k_ref[...], kp_ref[...], preferred_element_type=jnp.float32)
    side = me & 1
    k = me >> 1
    rows = other_ref.shape[1]
    for d in range(samps // 2):
        at = (k ^ d) * 2
        mine[d][...] = acc_ref[pl.ds(pl.multiple_of((at + side) * rows, rows), rows), :]
        other_ref[d] = acc_ref[pl.ds(pl.multiple_of((at + 1 - side) * rows, rows), rows), :]


def gram_kernel(me, pieces, kern_own, samples, norms, tile=512):
    samps = len(pieces)
    mc, ns = kern_own.shape
    width = samps * pieces[0].shape[0]
    inside = pl.BlockSpec(memory_space=pltpu.VMEM)
    shape = (mc // samps, width)
    return pl.pallas_call(
        functools.partial(gram_body, samps=samps, tile=tile),
        in_specs=[pl.BlockSpec(memory_space=pltpu.SMEM)] + [inside] * (samps + 3),
        out_specs=(inside,) * (2 + samps // 2),
        out_shape=(
            pltpu.VMEM((width, samples.shape[1]), jnp.bfloat16),
            pltpu.VMEM((samps // 2,) + shape, jnp.float32),
        )
        + (pltpu.VMEM(shape, jnp.float32),) * (samps // 2),
        scratch_shapes=[pltpu.VMEM((mc, width), jnp.float32), pltpu.VMEM((ns, width), jnp.bfloat16)],
        compiler_params=pltpu.CompilerParams(vmem_limit_bytes=16 << 20),
        name="gram",
    )(me, *[near(x) for x in pieces], kern_own, samples, norms)


from jax.sharding import PartitionSpec as P

PANEL = 512
GRAM_SCALE = 64.0


def swap(x, axis, d):
    n = lax.axis_size(axis)
    return lax.ppermute(x, axis, [(i, i ^ d) for i in range(n)])


def panel_pieces(centers):
    ctrs = lax.axis_size("ctr")
    samps = lax.axis_size("samp")
    rows = PANEL // samps
    chunk = lax.dynamic_slice_in_dim(centers, lax.axis_index("samp") * rows, rows, 0)
    got = [lax.ppermute(chunk, "ctr", [(0, d)]) for d in range(1, ctrs)]
    total = got[0]
    for piece in got[1:]:
        total = total + piece
    chunk = jnp.where(lax.axis_index("ctr") == 0, chunk, total)
    return [chunk] + [swap(chunk, "samp", d) for d in range(1, samps)]


def local(samples, centers):
    samp_count = lax.axis_size("samp")
    samp_index = lax.axis_index("samp").astype(jnp.int32)
    ctr_index = lax.axis_index("ctr").astype(jnp.int32)
    mc_dev = centers.shape[0]
    row_dev = mc_dev // samp_count
    me = samp_index.reshape(1)
    samples = near(samples)
    pieces = panel_pieces(centers)
    kern_own, norms, own = own_kernel(me, centers, samples, row_dev)
    panel, other, *mine = gram_kernel(me, pieces, kern_own, samples, norms)
    other = swap(other, "samp", 1)
    half = [mine[d] + other[d] for d in range(samp_count // 2)]
    total = half[0]
    for d in range(1, samp_count // 2):
        total = total + swap(half[d], "samp", 2 * d)
    gram = total * (GRAM_SCALE / (samples.shape[0] * samp_count))
    off = (ctr_index * mc_dev + samp_index * row_dev).reshape(1)
    chol, precond = chol_kernel(off, panel, own)
    return (gram[None], chol[None, :row_dev], precond)


def solution(mesh):
    placed = (P("samp", None), P("ctr", None))
    return jax.shard_map(
        local,
        mesh=mesh,
        in_specs=placed,
        out_specs=(P("ctr", "samp", None), P("ctr", "samp", None), P()),
        check_vma=False,
    )
```

```python
import functools
import jax, jax.numpy as jnp
from jax import lax
from jax.experimental import pallas as pl
from jax.experimental.pallas import tpu as pltpu
JITTER=0.01; SHIFT=0.5
RATIO=1.0/64
B=128
VB=32
HI=lax.Precision.HIGHEST
def mmul(a,b): return jnp.dot(a,b,preferred_element_type=jnp.float32,precision=HI)
def mmul_nt(a,b): return lax.dot_general(a,b,(((1,),(1,)),((),())),preferred_element_type=jnp.float32,precision=HI)
def lanebc(x,c): return jnp.broadcast_to(x[:,c:c+1],(8,B))
def subbc(x,j): return jnp.broadcast_to(x[j:j+1,:],(8,B))

def factor128(probs, fills=()):
    row=lax.broadcasted_iota(jnp.int32,(B,B),0)
    lane=lax.broadcasted_iota(jnp.int32,(B,B),1)
    n=VB//8
    for r,w,u,m in probs: w[...]=jnp.where(lane==row,1.0,0.0)
    for b in range(B//VB):
        base=b*VB
        st=[]
        for r,w,u,m in probs:
            st.append(([r[base+8*k:base+8*k+8,:] for k in range(n)],[w[base+8*k:base+8*k+8,:] for k in range(n)]))
        for i in range(n):
            loc=[]
            for X,Y in st:
                g=[lanebc(X[i],base+8*i+j) for j in range(8)]
                c={k:[lanebc(X[k],base+8*i+j) for j in range(8)] for k in range(i+1,n)}
                loc.append([g,c,X[i],Y[i]])
            for j in range(8):
                k=base+8*i+j
                for (r,w,u,m),(X,Y),L in zip(probs,st,loc):
                    g,c,a,y=L
                    rs=lax.rsqrt(subbc(g[j],j))
                    q=[None]*8
                    lj=g[j]*rs
                    for t in range(j+1,8):
                        q[t]=subbc(g[t],j)*rs
                        g[t]=g[t]-lj*q[t]
                    ur=subbc(a,j)*rs; wr=subbc(y,j)*rs
                    if j<7:
                        L[2]=a-lj*ur; L[3]=y-lj*wr
                    u[k:k+1,:]=ur[0:1]; m[k:k+1,:]=wr[0:1]
                    for z in range(i+1,n):
                        cj=c[z][j]*rs
                        for t in range(j+1,8): c[z][t]=c[z][t]-cj*q[t]
                        X[z]=X[z]-cj*ur; Y[z]=Y[z]-cj*wr
        e=base+VB
        if e<B:
            zs=[]
            for r,w,u,m in probs:
                ub=u[base:e,:]; mb=m[base:e,:]
                zs.append(mmul(ub.T[e:,:],jnp.concatenate([ub,mb],axis=1)))
            gaps=B//VB-1
            for f in fills[b::gaps]: f()
            for (r,w,u,m),z in zip(probs,zs):
                r[e:,:]=r[e:,:]-z[:,:B]
                w[e:,:]=w[e:,:]-z[:,B:]
    for r,w,u,m in probs: u[...]=jnp.where(lane>=row,u[...],0.0)

def kern_init(off_ref,panel_ref,own_ref,a_ref,nb,no):
    pan=panel_ref[...]; ow=own_ref[...]
    def bdot(a,b): return lax.dot_general(a,b,(((1,),(1,)),((),())),preferred_element_type=jnp.float32)
    c=-(2.0/panel_ref.shape[1])
    eye=lax.broadcasted_iota(jnp.int32,(B,B),0)==lax.broadcasted_iota(jnp.int32,(B,B),1)
    def diagrow(x):
        d=jnp.where(eye,x,0.0)
        return jnp.sum(d,axis=0,keepdims=True), jnp.sum(d,axis=1,keepdims=True)
    rows=[];cols=[]
    for i in range(nb):
        pi=pan[i*B:(i+1)*B]
        r,cc=diagrow(bdot(pi,pi)); rows.append(r); cols.append(cc)
    for i in range(no):
        oi=ow[i*B:(i+1)*B]
        r,_=diagrow(bdot(oi,oi)); rows.append(r)
    for i in range(nb):
        for j in range(nb+no):
            rhs=pan[j*B:(j+1)*B] if j<nb else ow[(j-nb)*B:(j-nb+1)*B]
            x=bdot(pan[i*B:(i+1)*B],rhs)
            k=jnp.exp(c*jnp.maximum(cols[i]+rows[j]-2.0*x,0.0))
            if j<nb:
                if i==j: k=k+jnp.where(eye,JITTER,0.0)
            else:
                gid=lax.broadcasted_iota(jnp.int32,(B,B),1)+(off_ref[0]+(j-nb)*B)
                k=k+jnp.where(gid==lax.broadcasted_iota(jnp.int32,(B,B),0)+i*B,JITTER,0.0)
            a_ref[i,j]=k

def put(M,uk,row,K,nb,u_ref,l_ref):
    un=mmul(M,jnp.concatenate(row,axis=1))
    for j in range(len(row)):
        v=un[:,j*B:(j+1)*B]
        if j<nb:
            v=jnp.where(j>K,v,0.0); v=jnp.where(j==K,uk,v)
        u_ref[K,j]=v
        l_ref[j,K]=v.T

def trail(a_ref,u_ref,l_ref,Kp,nb,nj):
    def one(i):
        z=mmul(l_ref[i,Kp],jnp.concatenate([u_ref[Kp,j] for j in range(i,nj)],axis=1))
        for j in range(i,nj):
            a_ref[i,j]=a_ref[i,j]-z[:,(j-i)*B:(j-i+1)*B]
    return [functools.partial(one,i) for i in range(1,nb)]

def init_body(off_ref,panel_ref,own_ref,a_ref,s_ref,*,own):
    nb=panel_ref.shape[0]//B; no=own//B
    kern_init(off_ref,panel_ref,own_ref,a_ref,nb,no)
    kr=[jnp.concatenate([a_ref[i,j] for j in range(nb)],axis=1) for i in range(nb)]
    kc=jnp.concatenate(kr,axis=0)
    for i in range(nb):
        z=mmul(kr[i],kc[:,i*B:])+SHIFT*kr[i][:,i*B:]
        for j in range(nb):
            s_ref[i,j]=z[:,(j-i)*B:(j-i+1)*B] if j>=i else jnp.zeros((B,B),jnp.float32)

def init_kernel(off,panel,own):
    ro=own.shape[0]; nb=panel.shape[0]//B; no=ro//B
    vm=pl.BlockSpec(memory_space=pltpu.VMEM)
    V=lambda *s: pltpu.VMEM(s+(B,B),jnp.float32)
    return pl.pallas_call(functools.partial(init_body,own=ro),
        out_shape=(V(nb,nb+no),V(nb,nb)),
        in_specs=[pl.BlockSpec(memory_space=pltpu.SMEM),vm,vm],out_specs=(vm,vm),
        compiler_params=pltpu.CompilerParams(vmem_limit_bytes=16<<20),
        name='kern_center')(off,panel,own)

def body(ain_ref,sin_ref,chol_ref,prec_ref,a_ref,u_ref,l_ref,s_ref,v_ref,h_ref,ms_ref,r0,w0,k0,m0,r1,w1,k1,m1):
    nb,nj=ain_ref.shape[:2]; no=nj-nb
    eye=lax.broadcasted_iota(jnp.int32,(B,B),0)==lax.broadcasted_iota(jnp.int32,(B,B),1)
    zero=jnp.zeros((B,B),jnp.float32)
    for j in range(nj):
        u_ref[nb,j]=zero; l_ref[j,nb]=zero
    for j in range(nb):
        v_ref[nb,j]=zero; h_ref[j,nb]=zero
    top=None
    for i in range(nb):
        for j in range(nj): a_ref[i,j]=ain_ref[i,j]
        for j in range(nb): s_ref[i,j]=sin_ref[i,j]
        d=jnp.where(eye,sin_ref[i,i],0.0)
        top=d if top is None else jnp.maximum(top,d)
    r0[...]=ain_ref[0,0]; r1[...]=sin_ref[0,0]
    def step(K,low):
        Kp=jnp.where(K==0,nb,K-1)
        fills=trail(a_ref,u_ref,l_ref,Kp,nb,nj)+trail(s_ref,v_ref,h_ref,Kp,nb,nb)[::-1]
        factor128([(r0,w0,k0,m0),(r1,w1,k1,m1)],fills)
        ms_ref[K]=m0[...]
        put(m0[...],k0[...],[a_ref[K,j] for j in range(nj)],K,nb,u_ref,l_ref)
        put(m1[...],k1[...],[s_ref[K,j] for j in range(nb)],K,nb,v_ref,h_ref)
        K1=jnp.minimum(K+1,nb-1)
        r0[...]=a_ref[K1,K1]-mmul(l_ref[K1,K],u_ref[K,K1])
        r1[...]=s_ref[K1,K1]-mmul(h_ref[K1,K],v_ref[K,K1])
        x=k1[...]
        return jnp.minimum(low,jnp.where(eye,x*x,1e30))
    low=lax.fori_loop(0,nb,step,jnp.full((B,B),1e30,jnp.float32))
    for i in range(no):
        for t in range(nb):
            chol_ref[i*B:(i+1)*B,t*B:(t+1)*B]=l_ref[nb+i,t]
    good=jnp.min(low)>=RATIO*jnp.max(top)
    @pl.when(good)
    def _():
        g=[]
        for K in range(nb):
            c=jnp.concatenate([h_ref[K,J] for J in range(K+1)],axis=1)
            for t in range(K):
                z=mmul(l_ref[K,t],g[t])
                c=jnp.concatenate([c[:,:(t+1)*B]-z,c[:,(t+1)*B:]],axis=1)
            g.append(mmul(ms_ref[K],c))
        for K in range(nb):
            for J in range(nb):
                prec_ref[K*B:(K+1)*B,J*B:(J+1)*B]=g[K][:,J*B:(J+1)*B] if J<=K else zero
    @pl.when(jnp.logical_not(good))
    def _():
        for C in range(nb):
            rows=[jnp.concatenate([u_ref[J,I] for I in range(C,nb)],axis=1) for J in range(C+1)]
            acc=mmul_nt(jnp.concatenate(rows,axis=0),rows[C])
            for J in range(C+1):
                v=acc[J*B:(J+1)*B]
                if J==C: v=v+jnp.where(eye,SHIFT,0.0)
                s_ref[J,C]=v
        for j in range(nb):
            v_ref[nb,j]=zero; h_ref[j,nb]=zero
        r1[...]=s_ref[0,0]
        def again(K,carry):
            Kp=jnp.where(K==0,nb,K-1)
            factor128([(r1,w1,k1,m1)],trail(s_ref,v_ref,h_ref,Kp,nb,nb))
            put(m1[...],k1[...],[s_ref[K,j] for j in range(nb)],K,nb,v_ref,h_ref)
            K1=jnp.minimum(K+1,nb-1)
            r1[...]=s_ref[K1,K1]-mmul(h_ref[K1,K],v_ref[K,K1])
            return carry
        lax.fori_loop(0,nb,again,0)
        for J in range(nb):
            for C in range(nb):
                prec_ref[J*B:(J+1)*B,C*B:(C+1)*B]=h_ref[J,C]

def factor_kernel(a,s):
    nb,nj=a.shape[:2]; no=nj-nb
    vm=pl.BlockSpec(memory_space=pltpu.VMEM)
    f32=jnp.float32
    V=lambda *s: pltpu.VMEM(s+(B,B),f32)
    return pl.pallas_call(body,
        out_shape=(jax.ShapeDtypeStruct((no*B,nb*B),f32),jax.ShapeDtypeStruct((nb*B,nb*B),f32)),
        in_specs=[vm,vm],out_specs=(vm,vm),
        scratch_shapes=[V(nb,nj),V(nb+1,nj),V(nj,nb+1),V(nb,nb),V(nb+1,nb),V(nb,nb+1),V(nb)]+[V()]*8,
        compiler_params=pltpu.CompilerParams(vmem_limit_bytes=24<<20),
        name='chol')(a,s)

def chol_kernel(off,panel,own):
    return factor_kernel(*init_kernel(off,panel,own))


LOG2E = 1.4426950408889634


def near(x):
    return pltpu.with_memory_space_constraint(x, pltpu.VMEM)


def far(x):
    return pltpu.with_memory_space_constraint(x, pltpu.HBM)


def square_parts(x):
    sq = jnp.square(x.astype(jnp.float32))
    hi = sq.astype(jnp.bfloat16)
    return hi, (sq - hi.astype(jnp.float32)).astype(jnp.bfloat16)


def nt(a, b):
    return lax.dot_general(a, b, (((1,), (1,)), ((), ())), preferred_element_type=jnp.float32)


def row_norms(x, scale):
    hi, lo = square_parts(x)
    one = jnp.ones((8, x.shape[1]), jnp.bfloat16)
    return (nt(one, hi) + nt(one, lo))[0:1] * scale


def col_norms(x, scale):
    hi, lo = square_parts(x)
    one = jnp.ones((x.shape[1], B), jnp.bfloat16)
    dot = lambda a: jnp.dot(a, one, preferred_element_type=jnp.float32)
    return (dot(hi) + dot(lo)) * scale


def kern_tile(x, y, xcol, yrow):
    dot = nt(x, y)
    both = jnp.concatenate([xcol] * (y.shape[0] // B), axis=1) + yrow
    arg = jnp.minimum(dot * (4.0 * LOG2E / x.shape[1]) + both, 0.0)
    return jnp.exp2(arg).astype(jnp.bfloat16)


def own_body(me_ref, c_hbm, s_hbm, k_ref, norm_ref, own_ref, s_ref, c_ref, c_sem, s_sem, *, row_dev, tile):
    scale = -2.0 * LOG2E / c_ref.shape[1]
    tiles = s_ref.shape[0] // tile
    first = pltpu.make_async_copy(c_hbm, c_ref, c_sem)
    first.start()
    copies = []
    for t in range(tiles):
        part = pl.ds(t * tile, tile)
        copies.append(pltpu.make_async_copy(s_hbm.at[part], s_ref.at[part], s_sem.at[t]))
        copies[-1].start()
    first.wait()
    at = pl.multiple_of(me_ref[0] * row_dev, row_dev)
    own_ref[0:row_dev, :] = c_ref[pl.ds(at, row_dev), :]
    if row_dev < own_ref.shape[0]:
        own_ref[row_dev:, :] = jnp.zeros((own_ref.shape[0] - row_dev, own_ref.shape[1]), own_ref.dtype)
    c = c_ref[...]
    ccol = col_norms(c, scale)
    for t in range(tiles):
        copies[t].wait()
        part = slice(t * tile, (t + 1) * tile)
        s = s_ref[part, :]
        norm_ref[part, :] = col_norms(s, scale)
        k_ref[:, part] = kern_tile(c, s, ccol, row_norms(s, scale))


def own_kernel(me, centers, samples, row_dev, tile=512):
    mc, d = centers.shape
    ns = samples.shape[0]
    inside = pl.BlockSpec(memory_space=pltpu.VMEM)
    outside = pl.BlockSpec(memory_space=pltpu.HBM)
    return pl.pallas_call(
        functools.partial(own_body, row_dev=row_dev, tile=tile),
        in_specs=[pl.BlockSpec(memory_space=pltpu.SMEM), outside, outside],
        out_specs=(inside,) * 4,
        out_shape=(
            pltpu.VMEM((mc, ns), jnp.bfloat16),
            pltpu.VMEM((ns, B), jnp.float32),
            pltpu.VMEM((row_dev + -row_dev % B, d), jnp.bfloat16),
            pltpu.VMEM((ns, d), jnp.bfloat16),
        ),
        scratch_shapes=[
            pltpu.VMEM((mc, d), jnp.bfloat16),
            pltpu.SemaphoreType.DMA(()),
            pltpu.SemaphoreType.DMA((ns // tile,)),
        ],
        compiler_params=pltpu.CompilerParams(vmem_limit_bytes=16 << 20),
        name="kern_own",
    )(me, far(centers), far(samples))


def gram_body(me_ref, *refs, samps, tile):
    pieces, (k_ref, s_ref, norm_ref) = refs[:samps], refs[samps : samps + 3]
    panel_ref, other_ref = refs[samps + 3 : samps + 5]
    mine, (acc_ref, kp_ref) = refs[samps + 5 : -2], refs[-2:]
    me = me_ref[0]
    rows = pieces[0].shape[0]
    for d in range(samps):
        panel_ref[pl.ds(pl.multiple_of((me ^ d) * rows, rows), rows), :] = pieces[d][...]
    panel = panel_ref[...]
    yrow = row_norms(panel, -2.0 * LOG2E / s_ref.shape[1])
    for t in range(0, s_ref.shape[0], tile):
        kp_ref[t : t + tile, :] = kern_tile(s_ref[t : t + tile, :], panel, norm_ref[t : t + tile, :], yrow)
    acc_ref[...] = jnp.dot(k_ref[...], kp_ref[...], preferred_element_type=jnp.float32)
    side = me & 1
    k = me >> 1
    rows = other_ref.shape[1]
    for d in range(samps // 2):
        at = (k ^ d) * 2
        mine[d][...] = acc_ref[pl.ds(pl.multiple_of((at + side) * rows, rows), rows), :]
        other_ref[d] = acc_ref[pl.ds(pl.multiple_of((at + 1 - side) * rows, rows), rows), :]


def gram_kernel(me, pieces, kern_own, samples, norms, tile=512):
    samps = len(pieces)
    mc, ns = kern_own.shape
    width = samps * pieces[0].shape[0]
    inside = pl.BlockSpec(memory_space=pltpu.VMEM)
    shape = (mc // samps, width)
    return pl.pallas_call(
        functools.partial(gram_body, samps=samps, tile=tile),
        in_specs=[pl.BlockSpec(memory_space=pltpu.SMEM)] + [inside] * (samps + 3),
        out_specs=(inside,) * (2 + samps // 2),
        out_shape=(
            pltpu.VMEM((width, samples.shape[1]), jnp.bfloat16),
            pltpu.VMEM((samps // 2,) + shape, jnp.float32),
        )
        + (pltpu.VMEM(shape, jnp.float32),) * (samps // 2),
        scratch_shapes=[pltpu.VMEM((mc, width), jnp.float32), pltpu.VMEM((ns, width), jnp.bfloat16)],
        compiler_params=pltpu.CompilerParams(vmem_limit_bytes=16 << 20),
        name="gram",
    )(me, *[near(x) for x in pieces], kern_own, samples, norms)


from jax.sharding import PartitionSpec as P

PANEL = 512
GRAM_SCALE = 64.0


def swap(x, axis, d):
    n = lax.axis_size(axis)
    return lax.ppermute(x, axis, [(i, i ^ d) for i in range(n)])


def panel_pieces(centers):
    ctrs = lax.axis_size("ctr")
    samps = lax.axis_size("samp")
    rows = PANEL // samps
    chunk = lax.dynamic_slice_in_dim(centers, lax.axis_index("samp") * rows, rows, 0)
    got = [lax.ppermute(chunk, "ctr", [(0, d)]) for d in range(1, ctrs)]
    total = got[0]
    for piece in got[1:]:
        total = total + piece
    chunk = jnp.where(lax.axis_index("ctr") == 0, chunk, total)
    return [chunk] + [swap(chunk, "samp", d) for d in range(1, samps)]


def local(samples, centers):
    samp_count = lax.axis_size("samp")
    samp_index = lax.axis_index("samp").astype(jnp.int32)
    ctr_index = lax.axis_index("ctr").astype(jnp.int32)
    mc_dev = centers.shape[0]
    row_dev = mc_dev // samp_count
    me = samp_index.reshape(1)
    pieces = panel_pieces(centers)
    kern_own, norms, own, held = own_kernel(me, centers, samples, row_dev)
    panel, other, *mine = gram_kernel(me, pieces, kern_own, held, norms)
    other = swap(other, "samp", 1)
    off = (ctr_index * mc_dev + samp_index * row_dev).reshape(1)
    first, second = init_kernel(off, panel, own)
    other, first, second = lax.optimization_barrier((other, first, second))
    half = [mine[d] + other[d] for d in range(samp_count // 2)]
    total = half[0]
    for d in range(1, samp_count // 2):
        total = total + swap(half[d], "samp", 2 * d)
    gram = total * (GRAM_SCALE / (samples.shape[0] * samp_count))
    chol, precond = factor_kernel(first, second)
    return (gram[None], chol[None, :row_dev], precond)


def solution(mesh):
    placed = (P("samp", None), P("ctr", None))
    return jax.shard_map(
        local,
        mesh=mesh,
        in_specs=placed,
        out_specs=(P("ctr", "samp", None), P("ctr", "samp", None), P()),
        check_vma=False,
    )
```

```python
import functools
import jax, jax.numpy as jnp
from jax import lax
from jax.experimental import pallas as pl
from jax.experimental.pallas import tpu as pltpu
JITTER=0.01; SHIFT=0.5
RATIO=1.0/64
B=128
VB=32
HI=lax.Precision.HIGHEST
def mmul(a,b): return jnp.dot(a,b,preferred_element_type=jnp.float32,precision=HI)
def mmul_nt(a,b): return lax.dot_general(a,b,(((1,),(1,)),((),())),preferred_element_type=jnp.float32,precision=HI)
def lanebc(x,c): return jnp.broadcast_to(x[:,c:c+1],(8,B))
def subbc(x,j): return jnp.broadcast_to(x[j:j+1,:],(8,B))

def factor128(probs, fills=()):
    row=lax.broadcasted_iota(jnp.int32,(B,B),0)
    lane=lax.broadcasted_iota(jnp.int32,(B,B),1)
    n=VB//8
    for r,w,u,m in probs: w[...]=jnp.where(lane==row,1.0,0.0)
    for b in range(B//VB):
        base=b*VB
        st=[]
        for r,w,u,m in probs:
            st.append(([r[base+8*k:base+8*k+8,:] for k in range(n)],[w[base+8*k:base+8*k+8,:] for k in range(n)]))
        for i in range(n):
            loc=[]
            for X,Y in st:
                g=[lanebc(X[i],base+8*i+j) for j in range(8)]
                c={k:[lanebc(X[k],base+8*i+j) for j in range(8)] for k in range(i+1,n)}
                loc.append([g,c,X[i],Y[i]])
            for j in range(8):
                k=base+8*i+j
                for (r,w,u,m),(X,Y),L in zip(probs,st,loc):
                    g,c,a,y=L
                    rs=lax.rsqrt(subbc(g[j],j))
                    q=[None]*8
                    lj=g[j]*rs
                    for t in range(j+1,8):
                        q[t]=subbc(g[t],j)*rs
                        g[t]=g[t]-lj*q[t]
                    ur=subbc(a,j)*rs; wr=subbc(y,j)*rs
                    if j<7:
                        L[2]=a-lj*ur; L[3]=y-lj*wr
                    u[k:k+1,:]=ur[0:1]; m[k:k+1,:]=wr[0:1]
                    for z in range(i+1,n):
                        cj=c[z][j]*rs
                        for t in range(j+1,8): c[z][t]=c[z][t]-cj*q[t]
                        X[z]=X[z]-cj*ur; Y[z]=Y[z]-cj*wr
        e=base+VB
        if e<B:
            zs=[]
            for r,w,u,m in probs:
                ub=u[base:e,:]; mb=m[base:e,:]
                zs.append(mmul(ub.T[e:,:],jnp.concatenate([ub,mb],axis=1)))
            gaps=B//VB-1
            for f in fills[b::gaps]: f()
            for (r,w,u,m),z in zip(probs,zs):
                r[e:,:]=r[e:,:]-z[:,:B]
                w[e:,:]=w[e:,:]-z[:,B:]
    for r,w,u,m in probs: u[...]=jnp.where(lane>=row,u[...],0.0)

def kern_init(off_ref,panel_ref,own_ref,a_ref,nb,no):
    pan=panel_ref[...]; ow=own_ref[...]
    def bdot(a,b): return lax.dot_general(a,b,(((1,),(1,)),((),())),preferred_element_type=jnp.float32)
    c=-(2.0/panel_ref.shape[1])
    eye=lax.broadcasted_iota(jnp.int32,(B,B),0)==lax.broadcasted_iota(jnp.int32,(B,B),1)
    def diagrow(x):
        d=jnp.where(eye,x,0.0)
        return jnp.sum(d,axis=0,keepdims=True), jnp.sum(d,axis=1,keepdims=True)
    rows=[];cols=[]
    for i in range(nb):
        pi=pan[i*B:(i+1)*B]
        r,cc=diagrow(bdot(pi,pi)); rows.append(r); cols.append(cc)
    for i in range(no):
        oi=ow[i*B:(i+1)*B]
        r,_=diagrow(bdot(oi,oi)); rows.append(r)
    for i in range(nb):
        for j in range(nb+no):
            rhs=pan[j*B:(j+1)*B] if j<nb else ow[(j-nb)*B:(j-nb+1)*B]
            x=bdot(pan[i*B:(i+1)*B],rhs)
            k=jnp.exp(c*jnp.maximum(cols[i]+rows[j]-2.0*x,0.0))
            if j<nb:
                if i==j: k=k+jnp.where(eye,JITTER,0.0)
            else:
                gid=lax.broadcasted_iota(jnp.int32,(B,B),1)+(off_ref[0]+(j-nb)*B)
                k=k+jnp.where(gid==lax.broadcasted_iota(jnp.int32,(B,B),0)+i*B,JITTER,0.0)
            a_ref[i,j]=k

def put(M,uk,row,K,nb,u_ref,l_ref):
    un=mmul(M,jnp.concatenate(row,axis=1))
    for j in range(len(row)):
        v=un[:,j*B:(j+1)*B]
        if j<nb:
            v=jnp.where(j>K,v,0.0); v=jnp.where(j==K,uk,v)
        u_ref[K,j]=v
        l_ref[j,K]=v.T

def trail(a_ref,u_ref,l_ref,Kp,nb,nj):
    def one(i):
        z=mmul(l_ref[i,Kp],jnp.concatenate([u_ref[Kp,j] for j in range(i,nj)],axis=1))
        for j in range(i,nj):
            a_ref[i,j]=a_ref[i,j]-z[:,(j-i)*B:(j-i+1)*B]
    return [functools.partial(one,i) for i in range(1,nb)]

def init_body(off_ref,panel_ref,own_ref,a_ref,s_ref,*,own):
    nb=panel_ref.shape[0]//B; no=own//B
    kern_init(off_ref,panel_ref,own_ref,a_ref,nb,no)
    kr=[jnp.concatenate([a_ref[i,j] for j in range(nb)],axis=1) for i in range(nb)]
    kc=jnp.concatenate(kr,axis=0)
    for i in range(nb):
        z=mmul(kr[i],kc[:,i*B:])+SHIFT*kr[i][:,i*B:]
        for j in range(nb):
            s_ref[i,j]=z[:,(j-i)*B:(j-i+1)*B] if j>=i else jnp.zeros((B,B),jnp.float32)

def init_kernel(off,panel,own):
    ro=own.shape[0]; nb=panel.shape[0]//B; no=ro//B
    vm=pl.BlockSpec(memory_space=pltpu.VMEM)
    V=lambda *s: pltpu.VMEM(s+(B,B),jnp.float32)
    return pl.pallas_call(functools.partial(init_body,own=ro),
        out_shape=(V(nb,nb+no),V(nb,nb)),
        in_specs=[pl.BlockSpec(memory_space=pltpu.SMEM),vm,vm],out_specs=(vm,vm),
        compiler_params=pltpu.CompilerParams(vmem_limit_bytes=16<<20),
        name='kern_center')(off,panel,own)

def body(ain_ref,sin_ref,chol_ref,prec_ref,a_ref,u_ref,l_ref,s_ref,v_ref,h_ref,ms_ref,r0,w0,k0,m0,r1,w1,k1,m1):
    nb,nj=ain_ref.shape[:2]; no=nj-nb
    eye=lax.broadcasted_iota(jnp.int32,(B,B),0)==lax.broadcasted_iota(jnp.int32,(B,B),1)
    zero=jnp.zeros((B,B),jnp.float32)
    for j in range(nj):
        u_ref[nb,j]=zero; l_ref[j,nb]=zero
    for j in range(nb):
        v_ref[nb,j]=zero; h_ref[j,nb]=zero
    top=None
    for i in range(nb):
        for j in range(nj): a_ref[i,j]=ain_ref[i,j]
        for j in range(nb): s_ref[i,j]=sin_ref[i,j]
        d=jnp.where(eye,sin_ref[i,i],0.0)
        top=d if top is None else jnp.maximum(top,d)
    r0[...]=ain_ref[0,0]; r1[...]=sin_ref[0,0]
    def step(K,low):
        Kp=jnp.where(K==0,nb,K-1)
        fills=trail(a_ref,u_ref,l_ref,Kp,nb,nj)+trail(s_ref,v_ref,h_ref,Kp,nb,nb)[::-1]
        factor128([(r0,w0,k0,m0),(r1,w1,k1,m1)],fills)
        ms_ref[K]=m0[...]
        put(m0[...],k0[...],[a_ref[K,j] for j in range(nj)],K,nb,u_ref,l_ref)
        put(m1[...],k1[...],[s_ref[K,j] for j in range(nb)],K,nb,v_ref,h_ref)
        K1=jnp.minimum(K+1,nb-1)
        r0[...]=a_ref[K1,K1]-mmul(l_ref[K1,K],u_ref[K,K1])
        r1[...]=s_ref[K1,K1]-mmul(h_ref[K1,K],v_ref[K,K1])
        x=k1[...]
        return jnp.minimum(low,jnp.where(eye,x*x,1e30))
    low=lax.fori_loop(0,nb,step,jnp.full((B,B),1e30,jnp.float32))
    for i in range(no):
        for t in range(nb):
            chol_ref[i*B:(i+1)*B,t*B:(t+1)*B]=l_ref[nb+i,t]
    good=jnp.min(low)>=RATIO*jnp.max(top)
    @pl.when(good)
    def _():
        g=[]
        for K in range(nb):
            c=jnp.concatenate([h_ref[K,J] for J in range(K+1)],axis=1)
            for t in range(K):
                z=mmul(l_ref[K,t],g[t])
                c=jnp.concatenate([c[:,:(t+1)*B]-z,c[:,(t+1)*B:]],axis=1)
            g.append(mmul(ms_ref[K],c))
        for K in range(nb):
            for J in range(nb):
                prec_ref[K*B:(K+1)*B,J*B:(J+1)*B]=g[K][:,J*B:(J+1)*B] if J<=K else zero
    @pl.when(jnp.logical_not(good))
    def _():
        for C in range(nb):
            rows=[jnp.concatenate([u_ref[J,I] for I in range(C,nb)],axis=1) for J in range(C+1)]
            acc=mmul_nt(jnp.concatenate(rows,axis=0),rows[C])
            for J in range(C+1):
                v=acc[J*B:(J+1)*B]
                if J==C: v=v+jnp.where(eye,SHIFT,0.0)
                s_ref[J,C]=v
        for j in range(nb):
            v_ref[nb,j]=zero; h_ref[j,nb]=zero
        r1[...]=s_ref[0,0]
        def again(K,carry):
            Kp=jnp.where(K==0,nb,K-1)
            factor128([(r1,w1,k1,m1)],trail(s_ref,v_ref,h_ref,Kp,nb,nb))
            put(m1[...],k1[...],[s_ref[K,j] for j in range(nb)],K,nb,v_ref,h_ref)
            K1=jnp.minimum(K+1,nb-1)
            r1[...]=s_ref[K1,K1]-mmul(h_ref[K1,K],v_ref[K,K1])
            return carry
        lax.fori_loop(0,nb,again,0)
        for J in range(nb):
            for C in range(nb):
                prec_ref[J*B:(J+1)*B,C*B:(C+1)*B]=h_ref[J,C]

def factor_kernel(a,s):
    nb,nj=a.shape[:2]; no=nj-nb
    vm=pl.BlockSpec(memory_space=pltpu.VMEM)
    f32=jnp.float32
    V=lambda *s: pltpu.VMEM(s+(B,B),f32)
    return pl.pallas_call(body,
        out_shape=(jax.ShapeDtypeStruct((no*B,nb*B),f32),jax.ShapeDtypeStruct((nb*B,nb*B),f32)),
        in_specs=[vm,vm],out_specs=(vm,vm),
        scratch_shapes=[V(nb,nj),V(nb+1,nj),V(nj,nb+1),V(nb,nb),V(nb+1,nb),V(nb,nb+1),V(nb)]+[V()]*8,
        compiler_params=pltpu.CompilerParams(vmem_limit_bytes=24<<20),
        name='chol')(a,s)

def chol_kernel(off,panel,own):
    return factor_kernel(*init_kernel(off,panel,own))


LOG2E = 1.4426950408889634


def near(x):
    return pltpu.with_memory_space_constraint(x, pltpu.VMEM)


def far(x):
    return pltpu.with_memory_space_constraint(x, pltpu.HBM)


def load_body(c_hbm, s_hbm, c_ref, s_ref, sem, *, parts):
    copies = []
    for t, (src, dst) in enumerate([(c_hbm, c_ref)] + [(s_hbm, s_ref)] * parts):
        rows = src.shape[0] // (parts if t else 1)
        part = pl.ds((t - 1) * rows if t else 0, rows)
        copies.append(pltpu.make_async_copy(src.at[part], dst.at[part], sem.at[t]))
        copies[-1].start()
    for copy in copies:
        copy.wait()


def load_kernel(centers, samples, parts=2):
    outside = pl.BlockSpec(memory_space=pltpu.HBM)
    inside = pl.BlockSpec(memory_space=pltpu.VMEM)
    return pl.pallas_call(
        functools.partial(load_body, parts=parts),
        in_specs=[outside, outside],
        out_specs=(inside, inside),
        out_shape=(pltpu.VMEM(centers.shape, centers.dtype), pltpu.VMEM(samples.shape, samples.dtype)),
        scratch_shapes=[pltpu.SemaphoreType.DMA((1 + parts,))],
        compiler_params=pltpu.CompilerParams(vmem_limit_bytes=4 << 20),
        name="load",
    )(far(centers), far(samples))


def pair_body(other_ref, *refs):
    n = len(refs) // 2
    for d in range(n):
        refs[n + d][...] = refs[d][...] + other_ref[d]


def pair_kernel(other, mine):
    inside = pl.BlockSpec(memory_space=pltpu.VMEM)
    return pl.pallas_call(
        pair_body,
        in_specs=[inside] * (1 + len(mine)),
        out_specs=[inside] * len(mine),
        out_shape=[pltpu.VMEM(x.shape, x.dtype) for x in mine],
        compiler_params=pltpu.CompilerParams(vmem_limit_bytes=4 << 20),
        name="pair_sum",
    )(near(other), *[near(x) for x in mine])


def total_body(*refs, scale):
    total = refs[0][...]
    for ref in refs[1:-1]:
        total = total + ref[...]
    refs[-1][...] = total * scale


def total_kernel(parts, scale):
    inside = pl.BlockSpec(memory_space=pltpu.VMEM)
    return pl.pallas_call(
        functools.partial(total_body, scale=scale),
        in_specs=[inside] * len(parts),
        out_specs=inside,
        out_shape=jax.ShapeDtypeStruct(parts[0].shape, parts[0].dtype),
        compiler_params=pltpu.CompilerParams(vmem_limit_bytes=4 << 20),
        name="gram_sum",
    )(*[near(x) for x in parts])


def square_parts(x):
    sq = jnp.square(x.astype(jnp.float32))
    hi = sq.astype(jnp.bfloat16)
    return hi, (sq - hi.astype(jnp.float32)).astype(jnp.bfloat16)


def nt(a, b):
    return lax.dot_general(a, b, (((1,), (1,)), ((), ())), preferred_element_type=jnp.float32)


def row_norms(x, scale):
    hi, lo = square_parts(x)
    one = jnp.ones((8, x.shape[1]), jnp.bfloat16)
    return (nt(one, hi) + nt(one, lo))[0:1] * scale


def col_norms(x, scale):
    hi, lo = square_parts(x)
    one = jnp.ones((x.shape[1], B), jnp.bfloat16)
    dot = lambda a: jnp.dot(a, one, preferred_element_type=jnp.float32)
    return (dot(hi) + dot(lo)) * scale


def kern_tile(x, y, xcol, yrow):
    dot = nt(x, y)
    both = jnp.concatenate([xcol] * (y.shape[0] // B), axis=1) + yrow
    arg = jnp.minimum(dot * (4.0 * LOG2E / x.shape[1]) + both, 0.0)
    return jnp.exp2(arg).astype(jnp.bfloat16)


def own_body(me_ref, c_ref, s_ref, k_ref, norm_ref, own_ref, *, row_dev):
    scale = -2.0 * LOG2E / c_ref.shape[1]
    at = pl.multiple_of(me_ref[0] * row_dev, row_dev)
    own_ref[0:row_dev, :] = c_ref[pl.ds(at, row_dev), :]
    if row_dev < own_ref.shape[0]:
        own_ref[row_dev:, :] = jnp.zeros((own_ref.shape[0] - row_dev, own_ref.shape[1]), own_ref.dtype)
    c = c_ref[...]
    ccol = col_norms(c, scale)
    tile = 2 * B
    for t in range(0, s_ref.shape[0], tile):
        s = s_ref[t : t + tile, :]
        norm_ref[t : t + tile, :] = col_norms(s, scale)
        k_ref[:, t : t + tile] = kern_tile(c, s, ccol, row_norms(s, scale))


def own_kernel(me, centers, samples, row_dev):
    mc, d = centers.shape
    ns = samples.shape[0]
    inside = pl.BlockSpec(memory_space=pltpu.VMEM)
    return pl.pallas_call(
        functools.partial(own_body, row_dev=row_dev),
        in_specs=[pl.BlockSpec(memory_space=pltpu.SMEM), inside, inside],
        out_specs=(inside, inside, inside),
        out_shape=(
            pltpu.VMEM((mc, ns), jnp.bfloat16),
            pltpu.VMEM((ns, B), jnp.float32),
            pltpu.VMEM((row_dev + -row_dev % B, d), jnp.bfloat16),
        ),
        compiler_params=pltpu.CompilerParams(vmem_limit_bytes=16 << 20),
        name="kern_own",
    )(me, centers, samples)


def gram_body(me_ref, *refs, samps, tile):
    pieces, (k_ref, s_ref, norm_ref) = refs[:samps], refs[samps : samps + 3]
    panel_ref, other_ref = refs[samps + 3 : samps + 5]
    mine, (acc_ref, kp_ref) = refs[samps + 5 : -2], refs[-2:]
    me = me_ref[0]
    rows = pieces[0].shape[0]
    for d in range(samps):
        panel_ref[pl.ds(pl.multiple_of((me ^ d) * rows, rows), rows), :] = pieces[d][...]
    panel = panel_ref[...]
    yrow = row_norms(panel, -2.0 * LOG2E / s_ref.shape[1])
    for t in range(0, s_ref.shape[0], tile):
        kp_ref[t : t + tile, :] = kern_tile(s_ref[t : t + tile, :], panel, norm_ref[t : t + tile, :], yrow)
    acc_ref[...] = jnp.dot(k_ref[...], kp_ref[...], preferred_element_type=jnp.float32)
    side = me & 1
    k = me >> 1
    rows = other_ref.shape[1]
    for d in range(samps // 2):
        at = (k ^ d) * 2
        mine[d][...] = acc_ref[pl.ds(pl.multiple_of((at + side) * rows, rows), rows), :]
        other_ref[d] = acc_ref[pl.ds(pl.multiple_of((at + 1 - side) * rows, rows), rows), :]


def gram_kernel(me, pieces, kern_own, samples, norms, tile=512):
    samps = len(pieces)
    mc, ns = kern_own.shape
    width = samps * pieces[0].shape[0]
    inside = pl.BlockSpec(memory_space=pltpu.VMEM)
    shape = (mc // samps, width)
    return pl.pallas_call(
        functools.partial(gram_body, samps=samps, tile=tile),
        in_specs=[pl.BlockSpec(memory_space=pltpu.SMEM)] + [inside] * (samps + 3),
        out_specs=(inside,) * (2 + samps // 2),
        out_shape=(
            pltpu.VMEM((width, samples.shape[1]), jnp.bfloat16),
            pltpu.VMEM((samps // 2,) + shape, jnp.float32),
        )
        + (pltpu.VMEM(shape, jnp.float32),) * (samps // 2),
        scratch_shapes=[pltpu.VMEM((mc, width), jnp.float32), pltpu.VMEM((ns, width), jnp.bfloat16)],
        compiler_params=pltpu.CompilerParams(vmem_limit_bytes=16 << 20),
        name="gram",
    )(me, *[near(x) for x in pieces], kern_own, samples, norms)


from jax.sharding import PartitionSpec as P

PANEL = 512
GRAM_SCALE = 64.0


def swap(x, axis, d):
    n = lax.axis_size(axis)
    return lax.ppermute(x, axis, [(i, i ^ d) for i in range(n)])


def panel_pieces(centers, samples):
    ctrs = lax.axis_size("ctr")
    samps = lax.axis_size("samp")
    rows = PANEL // samps
    chunk = lax.dynamic_slice_in_dim(centers, lax.axis_index("samp") * rows, rows, 0)
    got = [lax.ppermute(chunk, "ctr", [(0, d)]) for d in range(1, ctrs)]
    got, near_centers, near_samples = lax.optimization_barrier((got, *load_kernel(centers, samples)))
    total = got[0]
    for piece in got[1:]:
        total = total + piece
    chunk = jnp.where(lax.axis_index("ctr") == 0, chunk, total)
    return near_centers, near_samples, [chunk] + [swap(chunk, "samp", d) for d in range(1, samps)]


def local(samples, centers):
    samp_count = lax.axis_size("samp")
    samp_index = lax.axis_index("samp").astype(jnp.int32)
    ctr_index = lax.axis_index("ctr").astype(jnp.int32)
    mc_dev = centers.shape[0]
    row_dev = mc_dev // samp_count
    me = samp_index.reshape(1)
    near_centers, held, pieces = panel_pieces(centers, samples)
    kern_own, norms, own = own_kernel(me, near_centers, held, row_dev)
    panel, other, *mine = gram_kernel(me, pieces, kern_own, held, norms)
    other = swap(other, "samp", 1)
    off = (ctr_index * mc_dev + samp_index * row_dev).reshape(1)
    first, second = init_kernel(off, panel, own)
    other, first, second = lax.optimization_barrier((other, first, second))
    half = pair_kernel(other, mine)
    parts = [half[0]] + [swap(half[d], "samp", 2 * d) for d in range(1, samp_count // 2)]
    chol, precond = factor_kernel(first, second)
    gram = total_kernel(parts, GRAM_SCALE / (samples.shape[0] * samp_count))
    return (gram[None], chol[None, :row_dev], precond)


def solution(mesh):
    placed = (P("samp", None), P("ctr", None))
    return jax.shard_map(
        local,
        mesh=mesh,
        in_specs=placed,
        out_specs=(P("ctr", "samp", None), P("ctr", "samp", None), P()),
        check_vma=False,
    )
```

```python
import functools
import jax, jax.numpy as jnp
from jax import lax
from jax.experimental import pallas as pl
from jax.experimental.pallas import tpu as pltpu
JITTER=0.01; SHIFT=0.5
RATIO=1.0/64
B=128
VB=32
HI=lax.Precision.HIGHEST
def mmul(a,b): return jnp.dot(a,b,preferred_element_type=jnp.float32,precision=HI)
def mmul_nt(a,b): return lax.dot_general(a,b,(((1,),(1,)),((),())),preferred_element_type=jnp.float32,precision=HI)
def lanebc(x,c): return jnp.broadcast_to(x[:,c:c+1],(8,B))
def subbc(x,j): return jnp.broadcast_to(x[j:j+1,:],(8,B))

def factor128(probs, fills=()):
    row=lax.broadcasted_iota(jnp.int32,(B,B),0)
    lane=lax.broadcasted_iota(jnp.int32,(B,B),1)
    n=VB//8
    for r,w,u,m in probs: w[...]=jnp.where(lane==row,1.0,0.0)
    for b in range(B//VB):
        base=b*VB
        st=[]
        for r,w,u,m in probs:
            st.append(([r[base+8*k:base+8*k+8,:] for k in range(n)],[w[base+8*k:base+8*k+8,:] for k in range(n)]))
        for i in range(n):
            loc=[]
            for X,Y in st:
                g=[lanebc(X[i],base+8*i+j) for j in range(8)]
                c={k:[lanebc(X[k],base+8*i+j) for j in range(8)] for k in range(i+1,n)}
                loc.append([g,c,X[i],Y[i]])
            for j in range(8):
                k=base+8*i+j
                for (r,w,u,m),(X,Y),L in zip(probs,st,loc):
                    g,c,a,y=L
                    rs=lax.rsqrt(subbc(g[j],j))
                    q=[None]*8
                    lj=g[j]*rs
                    for t in range(j+1,8):
                        q[t]=subbc(g[t],j)*rs
                        g[t]=g[t]-lj*q[t]
                    ur=subbc(a,j)*rs; wr=subbc(y,j)*rs
                    if j<7:
                        L[2]=a-lj*ur; L[3]=y-lj*wr
                    u[k:k+1,:]=ur[0:1]; m[k:k+1,:]=wr[0:1]
                    for z in range(i+1,n):
                        cj=c[z][j]*rs
                        for t in range(j+1,8): c[z][t]=c[z][t]-cj*q[t]
                        X[z]=X[z]-cj*ur; Y[z]=Y[z]-cj*wr
        e=base+VB
        if e<B:
            zs=[]
            for r,w,u,m in probs:
                ub=u[base:e,:]; mb=m[base:e,:]
                zs.append(mmul(ub.T[e:,:],jnp.concatenate([ub,mb],axis=1)))
            for f in fills[b:b+1]: f()
            for (r,w,u,m),z in zip(probs,zs):
                r[e:,:]=r[e:,:]-z[:,:B]
                w[e:,:]=w[e:,:]-z[:,B:]
    for r,w,u,m in probs: u[...]=jnp.where(lane>=row,u[...],0.0)

def kern_init(off_ref,panel_ref,own_ref,a_ref,nb,no):
    pan=panel_ref[...]; ow=own_ref[...]
    def bdot(a,b): return lax.dot_general(a,b,(((1,),(1,)),((),())),preferred_element_type=jnp.float32)
    c=-(2.0/panel_ref.shape[1])
    eye=lax.broadcasted_iota(jnp.int32,(B,B),0)==lax.broadcasted_iota(jnp.int32,(B,B),1)
    def diagrow(x):
        d=jnp.where(eye,x,0.0)
        return jnp.sum(d,axis=0,keepdims=True), jnp.sum(d,axis=1,keepdims=True)
    rows=[];cols=[]
    for i in range(nb):
        pi=pan[i*B:(i+1)*B]
        r,cc=diagrow(bdot(pi,pi)); rows.append(r); cols.append(cc)
    for i in range(no):
        oi=ow[i*B:(i+1)*B]
        r,_=diagrow(bdot(oi,oi)); rows.append(r)
    for i in range(nb):
        for j in range(nb+no):
            rhs=pan[j*B:(j+1)*B] if j<nb else ow[(j-nb)*B:(j-nb+1)*B]
            x=bdot(pan[i*B:(i+1)*B],rhs)
            k=jnp.exp(c*jnp.maximum(cols[i]+rows[j]-2.0*x,0.0))
            if j<nb:
                if i==j: k=k+jnp.where(eye,JITTER,0.0)
            else:
                gid=lax.broadcasted_iota(jnp.int32,(B,B),1)+(off_ref[0]+(j-nb)*B)
                k=k+jnp.where(gid==lax.broadcasted_iota(jnp.int32,(B,B),0)+i*B,JITTER,0.0)
            a_ref[i,j]=k

def put(M,uk,row,K,nb,u_ref,l_ref):
    un=mmul(M,jnp.concatenate(row,axis=1))
    for j in range(len(row)):
        v=un[:,j*B:(j+1)*B]
        if j<nb:
            v=uk if isinstance(K,int) and j==K else jnp.where(j==K,uk,jnp.where(j>K,v,0.0))
        u_ref[K,j]=v
        l_ref[j,K]=v.T

def trail(a_ref,u_ref,l_ref,Kp,nb,nj):
    def one(i):
        z=mmul(l_ref[i,Kp],jnp.concatenate([u_ref[Kp,j] for j in range(i,nj)],axis=1))
        for j in range(i,nj):
            a_ref[i,j]=a_ref[i,j]-z[:,(j-i)*B:(j-i+1)*B]
    return [functools.partial(one,i) for i in range(1,nb)]

def init_body(off_ref,panel_ref,own_ref,a_ref,s_ref,*,own):
    nb=panel_ref.shape[0]//B; no=own//B
    kern_init(off_ref,panel_ref,own_ref,a_ref,nb,no)
    kr=[jnp.concatenate([a_ref[i,j] for j in range(nb)],axis=1) for i in range(nb)]
    kc=jnp.concatenate(kr,axis=0)
    for i in range(nb):
        z=mmul(kr[i],kc[:,i*B:])+SHIFT*kr[i][:,i*B:]
        for j in range(nb):
            s_ref[i,j]=z[:,(j-i)*B:(j-i+1)*B] if j>=i else jnp.zeros((B,B),jnp.float32)

def init_kernel(off,panel,own):
    ro=own.shape[0]; nb=panel.shape[0]//B; no=ro//B
    vm=pl.BlockSpec(memory_space=pltpu.VMEM)
    V=lambda *s: pltpu.VMEM(s+(B,B),jnp.float32)
    return pl.pallas_call(functools.partial(init_body,own=ro),
        out_shape=(V(nb,nb+no),V(nb,nb)),
        in_specs=[pl.BlockSpec(memory_space=pltpu.SMEM),vm,vm],out_specs=(vm,vm),
        compiler_params=pltpu.CompilerParams(vmem_limit_bytes=16<<20),
        name='kern_center')(off,panel,own)

def body(ain_ref,sin_ref,chol_ref,prec_ref,a_ref,u_ref,l_ref,s_ref,v_ref,h_ref,ms_ref,ks_ref,mc_ref,kc_ref,r0,w0,k0,m0,r1,w1,k1,m1):
    nb,nj=ain_ref.shape[:2]; no=nj-nb
    eye=lax.broadcasted_iota(jnp.int32,(B,B),0)==lax.broadcasted_iota(jnp.int32,(B,B),1)
    zero=jnp.zeros((B,B),jnp.float32)
    for j in range(nj):
        u_ref[nb,j]=zero; l_ref[j,nb]=zero; a_ref[nb,j]=zero
    for j in range(nb):
        v_ref[nb,j]=zero; h_ref[j,nb]=zero
    for j in range(nb): s_ref[nb,j]=zero
    for ref in (ms_ref,ks_ref,mc_ref,kc_ref): ref[nb]=zero
    top=None
    for i in range(nb):
        for j in range(nj): a_ref[i,j]=ain_ref[i,j]
        for j in range(nb): s_ref[i,j]=sin_ref[i,j]
        d=jnp.where(eye,sin_ref[i,i],0.0)
        top=d if top is None else jnp.maximum(top,d)
    r0[...]=ain_ref[0,0]; r1[...]=sin_ref[0,0]
    def step(K,low):
        Kp=jnp.where(K==0,nb,K-1)
        tl=trail(a_ref,u_ref,l_ref,Kp,nb,nj); tc=trail(s_ref,v_ref,h_ref,Kp,nb,nb)
        def rows():
            put(ms_ref[Kp],ks_ref[Kp],[a_ref[Kp,j] for j in range(nj)],Kp,nb,u_ref,l_ref)
            put(mc_ref[Kp],kc_ref[Kp],[s_ref[Kp,j] for j in range(nb)],Kp,nb,v_ref,h_ref)
        def run(fs):
            for f in fs: f()
        half=len(tl)//2+1
        factor128([(r0,w0,k0,m0),(r1,w1,k1,m1)],
            [rows,functools.partial(run,tl[:half]+tc[:half-1]),functools.partial(run,tl[half:]+tc[half-1:])])
        K1=jnp.minimum(K+1,nb-1)
        x0=mmul(m0[...],a_ref[K,K1]); x1=mmul(m1[...],s_ref[K,K1])
        r0[...]=a_ref[K1,K1]-mmul(x0.T,x0)
        r1[...]=s_ref[K1,K1]-mmul(x1.T,x1)
        ms_ref[K]=m0[...]; ks_ref[K]=k0[...]; mc_ref[K]=m1[...]; kc_ref[K]=k1[...]
        x=k1[...]
        return jnp.minimum(low,jnp.where(eye,x*x,1e30))
    low=lax.fori_loop(0,nb,step,jnp.full((B,B),1e30,jnp.float32))
    last=nb-1
    put(ms_ref[last],ks_ref[last],[a_ref[last,j] for j in range(nj)],last,nb,u_ref,l_ref)
    put(mc_ref[last],kc_ref[last],[s_ref[last,j] for j in range(nb)],last,nb,v_ref,h_ref)
    for i in range(no):
        for t in range(nb):
            chol_ref[i*B:(i+1)*B,t*B:(t+1)*B]=l_ref[nb+i,t]
    good=jnp.min(low)>=RATIO*jnp.max(top)
    @pl.when(good)
    def _():
        g=[]
        for K in range(nb):
            c=jnp.concatenate([h_ref[K,J] for J in range(K+1)],axis=1)
            for t in range(K):
                z=mmul(l_ref[K,t],g[t])
                c=jnp.concatenate([c[:,:(t+1)*B]-z,c[:,(t+1)*B:]],axis=1)
            g.append(mmul(ms_ref[K],c))
        for K in range(nb):
            for J in range(nb):
                prec_ref[K*B:(K+1)*B,J*B:(J+1)*B]=g[K][:,J*B:(J+1)*B] if J<=K else zero
    @pl.when(jnp.logical_not(good))
    def _():
        for C in range(nb):
            rows=[jnp.concatenate([u_ref[J,I] for I in range(C,nb)],axis=1) for J in range(C+1)]
            acc=mmul_nt(jnp.concatenate(rows,axis=0),rows[C])
            for J in range(C+1):
                v=acc[J*B:(J+1)*B]
                if J==C: v=v+jnp.where(eye,SHIFT,0.0)
                s_ref[J,C]=v
        for j in range(nb):
            v_ref[nb,j]=zero; h_ref[j,nb]=zero
        r1[...]=s_ref[0,0]
        def again(K,carry):
            Kp=jnp.where(K==0,nb,K-1)
            for f in trail(s_ref,v_ref,h_ref,Kp,nb,nb): f()
            factor128([(r1,w1,k1,m1)])
            put(m1[...],k1[...],[s_ref[K,j] for j in range(nb)],K,nb,v_ref,h_ref)
            K1=jnp.minimum(K+1,nb-1)
            r1[...]=s_ref[K1,K1]-mmul(h_ref[K1,K],v_ref[K,K1])
            return carry
        lax.fori_loop(0,nb,again,0)
        for J in range(nb):
            for C in range(nb):
                prec_ref[J*B:(J+1)*B,C*B:(C+1)*B]=h_ref[J,C]

def factor_kernel(a,s):
    nb,nj=a.shape[:2]; no=nj-nb
    vm=pl.BlockSpec(memory_space=pltpu.VMEM)
    f32=jnp.float32
    V=lambda *s: pltpu.VMEM(s+(B,B),f32)
    return pl.pallas_call(body,
        out_shape=(jax.ShapeDtypeStruct((no*B,nb*B),f32),jax.ShapeDtypeStruct((nb*B,nb*B),f32)),
        in_specs=[vm,vm],out_specs=(vm,vm),
        scratch_shapes=[V(nb+1,nj),V(nb+1,nj),V(nj,nb+1),V(nb+1,nb),V(nb+1,nb),V(nb,nb+1)]+[V(nb+1)]*4+[V()]*8,
        compiler_params=pltpu.CompilerParams(vmem_limit_bytes=24<<20),
        name='chol')(a,s)

def chol_kernel(off,panel,own):
    return factor_kernel(*init_kernel(off,panel,own))


LOG2E = 1.4426950408889634


def near(x):
    return pltpu.with_memory_space_constraint(x, pltpu.VMEM)


def far(x):
    return pltpu.with_memory_space_constraint(x, pltpu.HBM)


def load_body(c_hbm, s_hbm, c_ref, s_ref, sem, *, parts):
    copies = []
    for t, (src, dst) in enumerate([(c_hbm, c_ref)] + [(s_hbm, s_ref)] * parts):
        rows = src.shape[0] // (parts if t else 1)
        part = pl.ds((t - 1) * rows if t else 0, rows)
        copies.append(pltpu.make_async_copy(src.at[part], dst.at[part], sem.at[t]))
        copies[-1].start()
    for copy in copies:
        copy.wait()


def load_kernel(centers, samples, parts=2):
    outside = pl.BlockSpec(memory_space=pltpu.HBM)
    inside = pl.BlockSpec(memory_space=pltpu.VMEM)
    return pl.pallas_call(
        functools.partial(load_body, parts=parts),
        in_specs=[outside, outside],
        out_specs=(inside, inside),
        out_shape=(pltpu.VMEM(centers.shape, centers.dtype), pltpu.VMEM(samples.shape, samples.dtype)),
        scratch_shapes=[pltpu.SemaphoreType.DMA((1 + parts,))],
        compiler_params=pltpu.CompilerParams(vmem_limit_bytes=4 << 20),
        name="load",
    )(far(centers), far(samples))


def pair_body(other_ref, *refs):
    n = len(refs) // 2
    for d in range(n):
        refs[n + d][...] = refs[d][...] + other_ref[d]


def pair_kernel(other, mine):
    inside = pl.BlockSpec(memory_space=pltpu.VMEM)
    return pl.pallas_call(
        pair_body,
        in_specs=[inside] * (1 + len(mine)),
        out_specs=[inside] * len(mine),
        out_shape=[pltpu.VMEM(x.shape, x.dtype) for x in mine],
        compiler_params=pltpu.CompilerParams(vmem_limit_bytes=4 << 20),
        name="pair_sum",
    )(near(other), *[near(x) for x in mine])


def total_body(*refs, scale):
    total = refs[0][...]
    for ref in refs[1:-1]:
        total = total + ref[...]
    refs[-1][...] = total * scale


def total_kernel(parts, scale):
    inside = pl.BlockSpec(memory_space=pltpu.VMEM)
    return pl.pallas_call(
        functools.partial(total_body, scale=scale),
        in_specs=[inside] * len(parts),
        out_specs=inside,
        out_shape=jax.ShapeDtypeStruct(parts[0].shape, parts[0].dtype),
        compiler_params=pltpu.CompilerParams(vmem_limit_bytes=4 << 20),
        name="gram_sum",
    )(*[near(x) for x in parts])


def square_parts(x):
    sq = jnp.square(x.astype(jnp.float32))
    hi = sq.astype(jnp.bfloat16)
    return hi, (sq - hi.astype(jnp.float32)).astype(jnp.bfloat16)


def nt(a, b):
    return lax.dot_general(a, b, (((1,), (1,)), ((), ())), preferred_element_type=jnp.float32)


def row_norms(x, scale):
    hi, lo = square_parts(x)
    one = jnp.ones((8, x.shape[1]), jnp.bfloat16)
    return (nt(one, hi) + nt(one, lo))[0:1] * scale


def col_norms(x, scale):
    hi, lo = square_parts(x)
    one = jnp.ones((x.shape[1], B), jnp.bfloat16)
    dot = lambda a: jnp.dot(a, one, preferred_element_type=jnp.float32)
    return (dot(hi) + dot(lo)) * scale


def kern_tile(x, y, xcol, yrow):
    dot = nt(x, y)
    both = jnp.concatenate([xcol] * (y.shape[0] // B), axis=1) + yrow
    arg = jnp.minimum(dot * (4.0 * LOG2E / x.shape[1]) + both, 0.0)
    return jnp.exp2(arg).astype(jnp.bfloat16)


def own_body(me_ref, c_ref, s_ref, k_ref, norm_ref, own_ref, *, row_dev):
    scale = -2.0 * LOG2E / c_ref.shape[1]
    at = pl.multiple_of(me_ref[0] * row_dev, row_dev)
    own_ref[0:row_dev, :] = c_ref[pl.ds(at, row_dev), :]
    if row_dev < own_ref.shape[0]:
        own_ref[row_dev:, :] = jnp.zeros((own_ref.shape[0] - row_dev, own_ref.shape[1]), own_ref.dtype)
    c = c_ref[...]
    ccol = col_norms(c, scale)
    tile = 2 * B
    for t in range(0, s_ref.shape[0], tile):
        s = s_ref[t : t + tile, :]
        norm_ref[t : t + tile, :] = col_norms(s, scale)
        k_ref[:, t : t + tile] = kern_tile(c, s, ccol, row_norms(s, scale))


def own_kernel(me, centers, samples, row_dev):
    mc, d = centers.shape
    ns = samples.shape[0]
    inside = pl.BlockSpec(memory_space=pltpu.VMEM)
    return pl.pallas_call(
        functools.partial(own_body, row_dev=row_dev),
        in_specs=[pl.BlockSpec(memory_space=pltpu.SMEM), inside, inside],
        out_specs=(inside, inside, inside),
        out_shape=(
            pltpu.VMEM((mc, ns), jnp.bfloat16),
            pltpu.VMEM((ns, B), jnp.float32),
            pltpu.VMEM((row_dev + -row_dev % B, d), jnp.bfloat16),
        ),
        compiler_params=pltpu.CompilerParams(vmem_limit_bytes=16 << 20),
        name="kern_own",
    )(me, centers, samples)


def gram_body(me_ref, *refs, samps, tile):
    pieces, (k_ref, s_ref, norm_ref) = refs[:samps], refs[samps : samps + 3]
    panel_ref, other_ref = refs[samps + 3 : samps + 5]
    mine, (acc_ref, kp_ref) = refs[samps + 5 : -2], refs[-2:]
    me = me_ref[0]
    rows = pieces[0].shape[0]
    for d in range(samps):
        panel_ref[pl.ds(pl.multiple_of((me ^ d) * rows, rows), rows), :] = pieces[d][...]
    panel = panel_ref[...]
    yrow = row_norms(panel, -2.0 * LOG2E / s_ref.shape[1])
    for t in range(0, s_ref.shape[0], tile):
        kp_ref[t : t + tile, :] = kern_tile(s_ref[t : t + tile, :], panel, norm_ref[t : t + tile, :], yrow)
    acc_ref[...] = jnp.dot(k_ref[...], kp_ref[...], preferred_element_type=jnp.float32)
    side = me & 1
    k = me >> 1
    rows = other_ref.shape[1]
    for d in range(samps // 2):
        at = (k ^ d) * 2
        mine[d][...] = acc_ref[pl.ds(pl.multiple_of((at + side) * rows, rows), rows), :]
        other_ref[d] = acc_ref[pl.ds(pl.multiple_of((at + 1 - side) * rows, rows), rows), :]


def gram_kernel(me, pieces, kern_own, samples, norms, tile=512):
    samps = len(pieces)
    mc, ns = kern_own.shape
    width = samps * pieces[0].shape[0]
    inside = pl.BlockSpec(memory_space=pltpu.VMEM)
    shape = (mc // samps, width)
    return pl.pallas_call(
        functools.partial(gram_body, samps=samps, tile=tile),
        in_specs=[pl.BlockSpec(memory_space=pltpu.SMEM)] + [inside] * (samps + 3),
        out_specs=(inside,) * (2 + samps // 2),
        out_shape=(
            pltpu.VMEM((width, samples.shape[1]), jnp.bfloat16),
            pltpu.VMEM((samps // 2,) + shape, jnp.float32),
        )
        + (pltpu.VMEM(shape, jnp.float32),) * (samps // 2),
        scratch_shapes=[pltpu.VMEM((mc, width), jnp.float32), pltpu.VMEM((ns, width), jnp.bfloat16)],
        compiler_params=pltpu.CompilerParams(vmem_limit_bytes=16 << 20),
        name="gram",
    )(me, *[near(x) for x in pieces], kern_own, samples, norms)


from jax.sharding import PartitionSpec as P

PANEL = 512
GRAM_SCALE = 64.0


def swap(x, axis, d):
    n = lax.axis_size(axis)
    return lax.ppermute(x, axis, [(i, i ^ d) for i in range(n)])


def panel_pieces(centers, samples):
    ctrs = lax.axis_size("ctr")
    samps = lax.axis_size("samp")
    rows = PANEL // samps
    chunk = lax.dynamic_slice_in_dim(centers, lax.axis_index("samp") * rows, rows, 0)
    got = [lax.ppermute(chunk, "ctr", [(0, d)]) for d in range(1, ctrs)]
    got, near_centers, near_samples = lax.optimization_barrier((got, *load_kernel(centers, samples)))
    total = got[0]
    for piece in got[1:]:
        total = total + piece
    chunk = jnp.where(lax.axis_index("ctr") == 0, chunk, total)
    return near_centers, near_samples, [chunk] + [swap(chunk, "samp", d) for d in range(1, samps)]


def local(samples, centers):
    samp_count = lax.axis_size("samp")
    samp_index = lax.axis_index("samp").astype(jnp.int32)
    ctr_index = lax.axis_index("ctr").astype(jnp.int32)
    mc_dev = centers.shape[0]
    row_dev = mc_dev // samp_count
    me = samp_index.reshape(1)
    near_centers, held, pieces = panel_pieces(centers, samples)
    kern_own, norms, own = own_kernel(me, near_centers, held, row_dev)
    panel, other, *mine = gram_kernel(me, pieces, kern_own, held, norms)
    other = swap(other, "samp", 1)
    off = (ctr_index * mc_dev + samp_index * row_dev).reshape(1)
    first, second = init_kernel(off, panel, own)
    other, first, second = lax.optimization_barrier((other, first, second))
    half = pair_kernel(other, mine)
    parts = [half[0]] + [swap(half[d], "samp", 2 * d) for d in range(1, samp_count // 2)]
    chol, precond = factor_kernel(first, second)
    gram = total_kernel(parts, GRAM_SCALE / (samples.shape[0] * samp_count))
    return (gram[None], chol[None, :row_dev], precond)


def solution(mesh):
    placed = (P("samp", None), P("ctr", None))
    return jax.shard_map(
        local,
        mesh=mesh,
        in_specs=placed,
        out_specs=(P("ctr", "samp", None), P("ctr", "samp", None), P()),
        check_vma=False,
    )
```

```python
import functools
import jax, jax.numpy as jnp
from jax import lax
from jax.experimental import pallas as pl
from jax.experimental.pallas import tpu as pltpu
JITTER=0.01; SHIFT=0.5
RATIO=1.0/64
B=128
VB=32
HI=lax.Precision.HIGHEST
def mmul(a,b): return jnp.dot(a,b,preferred_element_type=jnp.float32,precision=HI)
def mmul_nt(a,b): return lax.dot_general(a,b,(((1,),(1,)),((),())),preferred_element_type=jnp.float32,precision=HI)
def lanebc(x,c): return jnp.broadcast_to(x[:,c:c+1],(8,B))
def subbc(x,j): return jnp.broadcast_to(x[j:j+1,:],(8,B))

def factor128(probs, fills=()):
    row=lax.broadcasted_iota(jnp.int32,(B,B),0)
    lane=lax.broadcasted_iota(jnp.int32,(B,B),1)
    n=VB//8
    for r,w,u,m in probs: w[...]=jnp.where(lane==row,1.0,0.0)
    for b in range(B//VB):
        base=b*VB
        st=[]
        for r,w,u,m in probs:
            st.append(([r[base+8*k:base+8*k+8,:] for k in range(n)],[w[base+8*k:base+8*k+8,:] for k in range(n)]))
        for i in range(n):
            loc=[]
            for X,Y in st:
                g=[lanebc(X[i],base+8*i+j) for j in range(8)]
                c={k:[lanebc(X[k],base+8*i+j) for j in range(8)] for k in range(i+1,n)}
                loc.append([g,c,X[i],Y[i]])
            for j in range(8):
                k=base+8*i+j
                for (r,w,u,m),(X,Y),L in zip(probs,st,loc):
                    g,c,a,y=L
                    rs=lax.rsqrt(subbc(g[j],j))
                    q=[None]*8
                    lj=g[j]*rs
                    for t in range(j+1,8):
                        q[t]=subbc(g[t],j)*rs
                        g[t]=g[t]-lj*q[t]
                    ur=subbc(a,j)*rs; wr=subbc(y,j)*rs
                    if j<7:
                        L[2]=a-lj*ur; L[3]=y-lj*wr
                    u[k:k+1,:]=ur[0:1]; m[k:k+1,:]=wr[0:1]
                    for z in range(i+1,n):
                        cj=c[z][j]*rs
                        for t in range(j+1,8): c[z][t]=c[z][t]-cj*q[t]
                        X[z]=X[z]-cj*ur; Y[z]=Y[z]-cj*wr
        e=base+VB
        if e<B:
            zs=[]
            for r,w,u,m in probs:
                ub=u[base:e,:]; mb=m[base:e,:]
                zs.append(mmul(ub.T[e:,:],jnp.concatenate([ub,mb],axis=1)))
            for f in fills[b:b+1]: f()
            for (r,w,u,m),z in zip(probs,zs):
                r[e:,:]=r[e:,:]-z[:,:B]
                w[e:,:]=w[e:,:]-z[:,B:]
    for r,w,u,m in probs: u[...]=jnp.where(lane>=row,u[...],0.0)

def kern_init(off_ref,panel_ref,own_ref,a_ref,nb,no):
    pan=panel_ref[...]; ow=own_ref[...]
    def bdot(a,b): return lax.dot_general(a,b,(((1,),(1,)),((),())),preferred_element_type=jnp.float32)
    c=-(2.0/panel_ref.shape[1])
    eye=lax.broadcasted_iota(jnp.int32,(B,B),0)==lax.broadcasted_iota(jnp.int32,(B,B),1)
    def diagrow(x):
        d=jnp.where(eye,x,0.0)
        return jnp.sum(d,axis=0,keepdims=True), jnp.sum(d,axis=1,keepdims=True)
    rows=[];cols=[]
    for i in range(nb):
        pi=pan[i*B:(i+1)*B]
        r,cc=diagrow(bdot(pi,pi)); rows.append(r); cols.append(cc)
    for i in range(no):
        oi=ow[i*B:(i+1)*B]
        r,_=diagrow(bdot(oi,oi)); rows.append(r)
    for i in range(nb):
        for j in range(nb+no):
            rhs=pan[j*B:(j+1)*B] if j<nb else ow[(j-nb)*B:(j-nb+1)*B]
            x=bdot(pan[i*B:(i+1)*B],rhs)
            k=jnp.exp(c*jnp.maximum(cols[i]+rows[j]-2.0*x,0.0))
            if j<nb:
                if i==j: k=k+jnp.where(eye,JITTER,0.0)
            else:
                gid=lax.broadcasted_iota(jnp.int32,(B,B),1)+(off_ref[0]+(j-nb)*B)
                k=k+jnp.where(gid==lax.broadcasted_iota(jnp.int32,(B,B),0)+i*B,JITTER,0.0)
            a_ref[i,j]=k

def put(M,uk,row,K,nb,u_ref,l_ref):
    un=mmul(M,jnp.concatenate(row,axis=1))
    for j in range(len(row)):
        v=un[:,j*B:(j+1)*B]
        if j<nb:
            v=uk if isinstance(K,int) and j==K else jnp.where(j==K,uk,jnp.where(j>K,v,0.0))
        u_ref[K,j]=v
        l_ref[j,K]=v.T

def trail(a_ref,u_ref,l_ref,Kp,nb,nj):
    def one(i):
        z=mmul(l_ref[i,Kp],jnp.concatenate([u_ref[Kp,j] for j in range(i,nj)],axis=1))
        for j in range(i,nj):
            a_ref[i,j]=a_ref[i,j]-z[:,(j-i)*B:(j-i+1)*B]
    return [functools.partial(one,i) for i in range(1,nb)]

def init_body(off_ref,panel_ref,own_ref,a_ref,s_ref,*,own):
    nb=panel_ref.shape[0]//B; no=own//B
    kern_init(off_ref,panel_ref,own_ref,a_ref,nb,no)
    kr=[jnp.concatenate([a_ref[i,j] for j in range(nb)],axis=1) for i in range(nb)]
    kc=jnp.concatenate(kr,axis=0)
    for i in range(nb):
        z=mmul(kr[i],kc[:,i*B:])+SHIFT*kr[i][:,i*B:]
        for j in range(nb):
            s_ref[i,j]=z[:,(j-i)*B:(j-i+1)*B] if j>=i else jnp.zeros((B,B),jnp.float32)

def init_kernel(off,panel,own):
    ro=own.shape[0]; nb=panel.shape[0]//B; no=ro//B
    vm=pl.BlockSpec(memory_space=pltpu.VMEM)
    V=lambda *s: pltpu.VMEM(s+(B,B),jnp.float32)
    return pl.pallas_call(functools.partial(init_body,own=ro),
        out_shape=(V(nb,nb+no),V(nb,nb)),
        in_specs=[pl.BlockSpec(memory_space=pltpu.SMEM),vm,vm],out_specs=(vm,vm),
        compiler_params=pltpu.CompilerParams(vmem_limit_bytes=16<<20),
        name='kern_center')(off,panel,own)

def body(ain_ref,sin_ref,chol_ref,prec_ref,a_ref,u_ref,l_ref,s_ref,v_ref,h_ref,ms_ref,ks_ref,mc_ref,kc_ref,r0,w0,k0,m0,r1,w1,k1,m1):
    nb,nj=ain_ref.shape[:2]; no=nj-nb
    eye=lax.broadcasted_iota(jnp.int32,(B,B),0)==lax.broadcasted_iota(jnp.int32,(B,B),1)
    zero=jnp.zeros((B,B),jnp.float32)
    for j in range(nj):
        u_ref[nb,j]=zero; l_ref[j,nb]=zero; a_ref[nb,j]=zero
    for j in range(nb):
        v_ref[nb,j]=zero; h_ref[j,nb]=zero
    for j in range(nb): s_ref[nb,j]=zero
    for ref in (ms_ref,ks_ref,mc_ref,kc_ref): ref[nb]=zero
    top=None
    for i in range(nb):
        for j in range(nj): a_ref[i,j]=ain_ref[i,j]
        for j in range(nb): s_ref[i,j]=sin_ref[i,j]
        d=jnp.where(eye,sin_ref[i,i],0.0)
        top=d if top is None else jnp.maximum(top,d)
    r0[...]=ain_ref[0,0]; r1[...]=sin_ref[0,0]
    def step(K,low):
        Kp=jnp.where(K==0,nb,K-1)
        tl=trail(a_ref,u_ref,l_ref,Kp,nb,nj); tc=trail(s_ref,v_ref,h_ref,Kp,nb,nb)
        def rows():
            put(ms_ref[Kp],ks_ref[Kp],[a_ref[Kp,j] for j in range(nj)],Kp,nb,u_ref,l_ref)
            put(mc_ref[Kp],kc_ref[Kp],[s_ref[Kp,j] for j in range(nb)],Kp,nb,v_ref,h_ref)
        def run(fs):
            for f in fs: f()
        half=len(tl)//2+1
        factor128([(r0,w0,k0,m0),(r1,w1,k1,m1)],
            [rows,functools.partial(run,tl[:half]+tc[:half-1]),functools.partial(run,tl[half:]+tc[half-1:])])
        K1=jnp.minimum(K+1,nb-1)
        x0=mmul(m0[...],a_ref[K,K1]); x1=mmul(m1[...],s_ref[K,K1])
        r0[...]=a_ref[K1,K1]-mmul(x0.T,x0)
        r1[...]=s_ref[K1,K1]-mmul(x1.T,x1)
        ms_ref[K]=m0[...]; ks_ref[K]=k0[...]; mc_ref[K]=m1[...]; kc_ref[K]=k1[...]
        x=k1[...]
        return jnp.minimum(low,jnp.where(eye,x*x,1e30))
    low=lax.fori_loop(0,nb,step,jnp.full((B,B),1e30,jnp.float32))
    last=nb-1
    put(ms_ref[last],ks_ref[last],[a_ref[last,j] for j in range(nj)],last,nb,u_ref,l_ref)
    put(mc_ref[last],kc_ref[last],[s_ref[last,j] for j in range(nb)],last,nb,v_ref,h_ref)
    for i in range(no):
        for t in range(nb):
            chol_ref[i*B:(i+1)*B,t*B:(t+1)*B]=l_ref[nb+i,t]
    good=jnp.min(low)>=RATIO*jnp.max(top)
    @pl.when(good)
    def _():
        g=[]
        for K in range(nb):
            c=jnp.concatenate([h_ref[K,J] for J in range(K+1)],axis=1)
            for t in range(K):
                z=mmul(l_ref[K,t],g[t])
                c=jnp.concatenate([c[:,:(t+1)*B]-z,c[:,(t+1)*B:]],axis=1)
            g.append(mmul(ms_ref[K],c))
        for K in range(nb):
            for J in range(nb):
                prec_ref[K*B:(K+1)*B,J*B:(J+1)*B]=g[K][:,J*B:(J+1)*B] if J<=K else zero
    @pl.when(jnp.logical_not(good))
    def _():
        for C in range(nb):
            rows=[jnp.concatenate([u_ref[J,I] for I in range(C,nb)],axis=1) for J in range(C+1)]
            acc=mmul_nt(jnp.concatenate(rows,axis=0),rows[C])
            for J in range(C+1):
                v=acc[J*B:(J+1)*B]
                if J==C: v=v+jnp.where(eye,SHIFT,0.0)
                s_ref[J,C]=v
        for j in range(nb):
            v_ref[nb,j]=zero; h_ref[j,nb]=zero
        r1[...]=s_ref[0,0]
        def again(K,carry):
            Kp=jnp.where(K==0,nb,K-1)
            for f in trail(s_ref,v_ref,h_ref,Kp,nb,nb): f()
            factor128([(r1,w1,k1,m1)])
            put(m1[...],k1[...],[s_ref[K,j] for j in range(nb)],K,nb,v_ref,h_ref)
            K1=jnp.minimum(K+1,nb-1)
            r1[...]=s_ref[K1,K1]-mmul(h_ref[K1,K],v_ref[K,K1])
            return carry
        lax.fori_loop(0,nb,again,0)
        for J in range(nb):
            for C in range(nb):
                prec_ref[J*B:(J+1)*B,C*B:(C+1)*B]=h_ref[J,C]

def factor_kernel(a,s):
    nb,nj=a.shape[:2]; no=nj-nb
    vm=pl.BlockSpec(memory_space=pltpu.VMEM)
    f32=jnp.float32
    V=lambda *s: pltpu.VMEM(s+(B,B),f32)
    return pl.pallas_call(body,
        out_shape=(jax.ShapeDtypeStruct((no*B,nb*B),f32),jax.ShapeDtypeStruct((nb*B,nb*B),f32)),
        in_specs=[vm,vm],out_specs=(vm,vm),
        scratch_shapes=[V(nb+1,nj),V(nb+1,nj),V(nj,nb+1),V(nb+1,nb),V(nb+1,nb),V(nb,nb+1)]+[V(nb+1)]*4+[V()]*8,
        compiler_params=pltpu.CompilerParams(vmem_limit_bytes=24<<20),
        name='chol')(a,s)

def chol_kernel(off,panel,own):
    return factor_kernel(*init_kernel(off,panel,own))


LOG2E = 1.4426950408889634


def near(x):
    return pltpu.with_memory_space_constraint(x, pltpu.VMEM)


def far(x):
    return pltpu.with_memory_space_constraint(x, pltpu.HBM)


def load_body(c_hbm, s_hbm, c_ref, s_ref, sem, *, parts):
    copies = []
    for t, (src, dst) in enumerate([(c_hbm, c_ref)] + [(s_hbm, s_ref)] * parts):
        rows = src.shape[0] // (parts if t else 1)
        part = pl.ds((t - 1) * rows if t else 0, rows)
        copies.append(pltpu.make_async_copy(src.at[part], dst.at[part], sem.at[t]))
        copies[-1].start()
    for copy in copies:
        copy.wait()


def load_kernel(centers, samples, parts=2):
    outside = pl.BlockSpec(memory_space=pltpu.HBM)
    inside = pl.BlockSpec(memory_space=pltpu.VMEM)
    return pl.pallas_call(
        functools.partial(load_body, parts=parts),
        in_specs=[outside, outside],
        out_specs=(inside, inside),
        out_shape=(pltpu.VMEM(centers.shape, centers.dtype), pltpu.VMEM(samples.shape, samples.dtype)),
        scratch_shapes=[pltpu.SemaphoreType.DMA((1 + parts,))],
        compiler_params=pltpu.CompilerParams(vmem_limit_bytes=4 << 20),
        name="load",
    )(far(centers), far(samples))


def pair_body(other_ref, *refs):
    n = len(refs) // 2
    for d in range(n):
        refs[n + d][...] = refs[d][...] + other_ref[d]


def pair_kernel(other, mine):
    inside = pl.BlockSpec(memory_space=pltpu.VMEM)
    return pl.pallas_call(
        pair_body,
        in_specs=[inside] * (1 + len(mine)),
        out_specs=[inside] * len(mine),
        out_shape=[pltpu.VMEM(x.shape, x.dtype) for x in mine],
        compiler_params=pltpu.CompilerParams(vmem_limit_bytes=4 << 20),
        name="pair_sum",
    )(near(other), *[near(x) for x in mine])


def total_body(*refs, scale):
    total = refs[0][...]
    for ref in refs[1:-1]:
        total = total + ref[...]
    refs[-1][...] = total * scale


def total_kernel(parts, scale):
    inside = pl.BlockSpec(memory_space=pltpu.VMEM)
    return pl.pallas_call(
        functools.partial(total_body, scale=scale),
        in_specs=[inside] * len(parts),
        out_specs=inside,
        out_shape=jax.ShapeDtypeStruct(parts[0].shape, parts[0].dtype),
        compiler_params=pltpu.CompilerParams(vmem_limit_bytes=4 << 20),
        name="gram_sum",
    )(*[near(x) for x in parts])


def square_parts(x):
    sq = jnp.square(x.astype(jnp.float32))
    hi = sq.astype(jnp.bfloat16)
    return hi, (sq - hi.astype(jnp.float32)).astype(jnp.bfloat16)


def nt(a, b):
    return lax.dot_general(a, b, (((1,), (1,)), ((), ())), preferred_element_type=jnp.float32)


def row_norms(x, scale):
    hi, lo = square_parts(x)
    one = jnp.ones((8, x.shape[1]), jnp.bfloat16)
    return (nt(one, hi) + nt(one, lo))[0:1] * scale


def col_norms(x, scale):
    total = jnp.sum(jnp.square(x.astype(jnp.float32)), axis=1, keepdims=True) * scale
    return jnp.broadcast_to(total, (x.shape[0], B))


def kern_tile(x, y, xcol, yrow):
    dot = nt(x, y)
    both = jnp.concatenate([xcol] * (y.shape[0] // B), axis=1) + yrow
    arg = jnp.minimum(dot * (4.0 * LOG2E / x.shape[1]) + both, 0.0)
    return jnp.exp2(arg).astype(jnp.bfloat16)


def own_body(me_ref, c_ref, s_ref, k_ref, norm_ref, own_ref, *, row_dev):
    scale = -2.0 * LOG2E / c_ref.shape[1]
    at = pl.multiple_of(me_ref[0] * row_dev, row_dev)
    own_ref[0:row_dev, :] = c_ref[pl.ds(at, row_dev), :]
    if row_dev < own_ref.shape[0]:
        own_ref[row_dev:, :] = jnp.zeros((own_ref.shape[0] - row_dev, own_ref.shape[1]), own_ref.dtype)
    c = c_ref[...]
    ccol = col_norms(c, scale)
    tile = 2 * B
    for t in range(0, s_ref.shape[0], tile):
        s = s_ref[t : t + tile, :]
        norm_ref[t : t + tile, :] = col_norms(s, scale)
        k_ref[:, t : t + tile] = kern_tile(c, s, ccol, row_norms(s, scale))


def own_kernel(me, centers, samples, row_dev):
    mc, d = centers.shape
    ns = samples.shape[0]
    inside = pl.BlockSpec(memory_space=pltpu.VMEM)
    return pl.pallas_call(
        functools.partial(own_body, row_dev=row_dev),
        in_specs=[pl.BlockSpec(memory_space=pltpu.SMEM), inside, inside],
        out_specs=(inside, inside, inside),
        out_shape=(
            pltpu.VMEM((mc, ns), jnp.bfloat16),
            pltpu.VMEM((ns, B), jnp.float32),
            pltpu.VMEM((row_dev + -row_dev % B, d), jnp.bfloat16),
        ),
        compiler_params=pltpu.CompilerParams(vmem_limit_bytes=16 << 20),
        name="kern_own",
    )(me, centers, samples)


def gram_body(me_ref, *refs, samps, tile):
    pieces, (k_ref, s_ref, norm_ref) = refs[:samps], refs[samps : samps + 3]
    panel_ref, other_ref = refs[samps + 3 : samps + 5]
    mine, (acc_ref, kp_ref) = refs[samps + 5 : -2], refs[-2:]
    me = me_ref[0]
    rows = pieces[0].shape[0]
    for d in range(samps):
        panel_ref[pl.ds(pl.multiple_of((me ^ d) * rows, rows), rows), :] = pieces[d][...]
    panel = panel_ref[...]
    yrow = row_norms(panel, -2.0 * LOG2E / s_ref.shape[1])
    for t in range(0, s_ref.shape[0], tile):
        kp_ref[t : t + tile, :] = kern_tile(s_ref[t : t + tile, :], panel, norm_ref[t : t + tile, :], yrow)
    acc_ref[...] = jnp.dot(k_ref[...], kp_ref[...], preferred_element_type=jnp.float32)
    side = me & 1
    k = me >> 1
    rows = other_ref.shape[1]
    for d in range(samps // 2):
        at = (k ^ d) * 2
        mine[d][...] = acc_ref[pl.ds(pl.multiple_of((at + side) * rows, rows), rows), :]
        other_ref[d] = acc_ref[pl.ds(pl.multiple_of((at + 1 - side) * rows, rows), rows), :]


def gram_kernel(me, pieces, kern_own, samples, norms, tile=512):
    samps = len(pieces)
    mc, ns = kern_own.shape
    width = samps * pieces[0].shape[0]
    inside = pl.BlockSpec(memory_space=pltpu.VMEM)
    shape = (mc // samps, width)
    return pl.pallas_call(
        functools.partial(gram_body, samps=samps, tile=tile),
        in_specs=[pl.BlockSpec(memory_space=pltpu.SMEM)] + [inside] * (samps + 3),
        out_specs=(inside,) * (2 + samps // 2),
        out_shape=(
            pltpu.VMEM((width, samples.shape[1]), jnp.bfloat16),
            pltpu.VMEM((samps // 2,) + shape, jnp.float32),
        )
        + (pltpu.VMEM(shape, jnp.float32),) * (samps // 2),
        scratch_shapes=[pltpu.VMEM((mc, width), jnp.float32), pltpu.VMEM((ns, width), jnp.bfloat16)],
        compiler_params=pltpu.CompilerParams(vmem_limit_bytes=16 << 20),
        name="gram",
    )(me, *[near(x) for x in pieces], kern_own, samples, norms)


from jax.sharding import PartitionSpec as P

PANEL = 512
GRAM_SCALE = 64.0


def swap(x, axis, d):
    n = lax.axis_size(axis)
    return lax.ppermute(x, axis, [(i, i ^ d) for i in range(n)])


def panel_pieces(centers, samples):
    ctrs = lax.axis_size("ctr")
    samps = lax.axis_size("samp")
    rows = PANEL // samps
    chunk = lax.dynamic_slice_in_dim(centers, lax.axis_index("samp") * rows, rows, 0)
    got = [lax.ppermute(chunk, "ctr", [(0, d)]) for d in range(1, ctrs)]
    got, near_centers, near_samples = lax.optimization_barrier((got, *load_kernel(centers, samples)))
    total = got[0]
    for piece in got[1:]:
        total = total + piece
    chunk = jnp.where(lax.axis_index("ctr") == 0, chunk, total)
    return near_centers, near_samples, [chunk] + [swap(chunk, "samp", d) for d in range(1, samps)]


def local(samples, centers):
    samp_count = lax.axis_size("samp")
    samp_index = lax.axis_index("samp").astype(jnp.int32)
    ctr_index = lax.axis_index("ctr").astype(jnp.int32)
    mc_dev = centers.shape[0]
    row_dev = mc_dev // samp_count
    me = samp_index.reshape(1)
    near_centers, held, pieces = panel_pieces(centers, samples)
    kern_own, norms, own = own_kernel(me, near_centers, held, row_dev)
    panel, other, *mine = gram_kernel(me, pieces, kern_own, held, norms)
    other = swap(other, "samp", 1)
    off = (ctr_index * mc_dev + samp_index * row_dev).reshape(1)
    first, second = init_kernel(off, panel, own)
    other, first, second = lax.optimization_barrier((other, first, second))
    half = pair_kernel(other, mine)
    parts = [half[0]] + [swap(half[d], "samp", 2 * d) for d in range(1, samp_count // 2)]
    chol, precond = factor_kernel(first, second)
    gram = total_kernel(parts, GRAM_SCALE / (samples.shape[0] * samp_count))
    return (gram[None], chol[None, :row_dev], precond)


def solution(mesh):
    placed = (P("samp", None), P("ctr", None))
    return jax.shard_map(
        local,
        mesh=mesh,
        in_specs=placed,
        out_specs=(P("ctr", "samp", None), P("ctr", "samp", None), P()),
        check_vma=False,
    )
```

```python
import functools
import jax, jax.numpy as jnp
from jax import lax
from jax.experimental import pallas as pl
from jax.experimental.pallas import tpu as pltpu
JITTER=0.01; SHIFT=0.5
RATIO=1.0/64
B=128
VB=32
HI=lax.Precision.HIGHEST
def mmul(a,b): return jnp.dot(a,b,preferred_element_type=jnp.float32,precision=HI)
def mmul_nt(a,b): return lax.dot_general(a,b,(((1,),(1,)),((),())),preferred_element_type=jnp.float32,precision=HI)
def lanebc(x,c): return jnp.broadcast_to(x[:,c:c+1],(8,B))
def subbc(x,j): return jnp.broadcast_to(x[j:j+1,:],(8,B))

def factor128(probs, fills=()):
    row=lax.broadcasted_iota(jnp.int32,(B,B),0)
    lane=lax.broadcasted_iota(jnp.int32,(B,B),1)
    n=VB//8
    for r,w,u,m in probs: w[...]=jnp.where(lane==row,1.0,0.0)
    for b in range(B//VB):
        base=b*VB
        st=[]
        for r,w,u,m in probs:
            st.append(([r[base+8*k:base+8*k+8,:] for k in range(n)],[w[base+8*k:base+8*k+8,:] for k in range(n)]))
        for i in range(n):
            loc=[]
            for X,Y in st:
                g=[lanebc(X[i],base+8*i+j) for j in range(8)]
                c={k:[lanebc(X[k],base+8*i+j) for j in range(8)] for k in range(i+1,n)}
                loc.append([g,c,X[i],Y[i]])
            for j in range(8):
                k=base+8*i+j
                for (r,w,u,m),(X,Y),L in zip(probs,st,loc):
                    g,c,a,y=L
                    rs=lax.rsqrt(subbc(g[j],j))
                    q=[None]*8
                    lj=g[j]*rs
                    for t in range(j+1,8):
                        q[t]=subbc(g[t],j)*rs
                        g[t]=g[t]-lj*q[t]
                    ur=subbc(a,j)*rs; wr=subbc(y,j)*rs
                    if j<7:
                        L[2]=a-lj*ur; L[3]=y-lj*wr
                    u[k:k+1,:]=ur[0:1]; m[k:k+1,:]=wr[0:1]
                    for z in range(i+1,n):
                        cj=c[z][j]*rs
                        for t in range(j+1,8): c[z][t]=c[z][t]-cj*q[t]
                        X[z]=X[z]-cj*ur; Y[z]=Y[z]-cj*wr
        e=base+VB
        if e<B:
            zs=[]
            for r,w,u,m in probs:
                ub=u[base:e,:]; mb=m[base:e,:]
                zs.append(mmul(ub.T[e:,:],jnp.concatenate([ub,mb],axis=1)))
            for f in fills[b:b+1]: f()
            for (r,w,u,m),z in zip(probs,zs):
                r[e:,:]=r[e:,:]-z[:,:B]
                w[e:,:]=w[e:,:]-z[:,B:]
    for r,w,u,m in probs: u[...]=jnp.where(lane>=row,u[...],0.0)

def kern_init(off_ref,panel_ref,own_ref,a_ref,nb,no):
    pan=panel_ref[...]; ow=own_ref[...]
    def bdot(a,b): return lax.dot_general(a,b,(((1,),(1,)),((),())),preferred_element_type=jnp.float32)
    c=-(2.0/panel_ref.shape[1])
    eye=lax.broadcasted_iota(jnp.int32,(B,B),0)==lax.broadcasted_iota(jnp.int32,(B,B),1)
    def diagrow(x):
        d=jnp.where(eye,x,0.0)
        return jnp.sum(d,axis=0,keepdims=True), jnp.sum(d,axis=1,keepdims=True)
    rows=[];cols=[]
    for i in range(nb):
        pi=pan[i*B:(i+1)*B]
        r,cc=diagrow(bdot(pi,pi)); rows.append(r); cols.append(cc)
    for i in range(no):
        oi=ow[i*B:(i+1)*B]
        r,_=diagrow(bdot(oi,oi)); rows.append(r)
    for i in range(nb):
        for j in range(nb+no):
            rhs=pan[j*B:(j+1)*B] if j<nb else ow[(j-nb)*B:(j-nb+1)*B]
            x=bdot(pan[i*B:(i+1)*B],rhs)
            k=jnp.exp(c*jnp.maximum(cols[i]+rows[j]-2.0*x,0.0))
            if j<nb:
                if i==j: k=k+jnp.where(eye,JITTER,0.0)
            else:
                gid=lax.broadcasted_iota(jnp.int32,(B,B),1)+(off_ref[0]+(j-nb)*B)
                k=k+jnp.where(gid==lax.broadcasted_iota(jnp.int32,(B,B),0)+i*B,JITTER,0.0)
            a_ref[i,j]=k

def put(M,uk,row,K,nb,u_ref,l_ref):
    un=mmul(M,jnp.concatenate(row,axis=1))
    for j in range(len(row)):
        v=un[:,j*B:(j+1)*B]
        if j<nb:
            v=uk if isinstance(K,int) and j==K else jnp.where(j==K,uk,jnp.where(j>K,v,0.0))
        u_ref[K,j]=v
        l_ref[j,K]=v.T

def trail(a_ref,u_ref,l_ref,Kp,nb,nj):
    def one(i):
        z=mmul(l_ref[i,Kp],jnp.concatenate([u_ref[Kp,j] for j in range(i,nj)],axis=1))
        for j in range(i,nj):
            a_ref[i,j]=a_ref[i,j]-z[:,(j-i)*B:(j-i+1)*B]
    return [functools.partial(one,i) for i in range(1,nb)]

def init_body(off_ref,panel_ref,own_ref,a_ref,s_ref,*,own):
    nb=panel_ref.shape[0]//B; no=own//B
    kern_init(off_ref,panel_ref,own_ref,a_ref,nb,no)
    kr=[jnp.concatenate([a_ref[i,j] for j in range(nb)],axis=1) for i in range(nb)]
    kc=jnp.concatenate(kr,axis=0)
    for i in range(nb):
        z=mmul(kr[i],kc[:,i*B:])+SHIFT*kr[i][:,i*B:]
        for j in range(nb):
            s_ref[i,j]=z[:,(j-i)*B:(j-i+1)*B] if j>=i else jnp.zeros((B,B),jnp.float32)

def init_kernel(off,panel,own):
    ro=own.shape[0]; nb=panel.shape[0]//B; no=ro//B
    vm=pl.BlockSpec(memory_space=pltpu.VMEM)
    V=lambda *s: pltpu.VMEM(s+(B,B),jnp.float32)
    return pl.pallas_call(functools.partial(init_body,own=ro),
        out_shape=(V(nb,nb+no),V(nb,nb)),
        in_specs=[pl.BlockSpec(memory_space=pltpu.SMEM),vm,vm],out_specs=(vm,vm),
        compiler_params=pltpu.CompilerParams(vmem_limit_bytes=16<<20),
        name='kern_center')(off,panel,own)

def body(ain_ref,sin_ref,chol_ref,prec_ref,a_ref,u_ref,l_ref,s_ref,v_ref,h_ref,ms_ref,ks_ref,mc_ref,kc_ref,r0,w0,k0,m0,r1,w1,k1,m1):
    nb,nj=ain_ref.shape[:2]; no=nj-nb
    eye=lax.broadcasted_iota(jnp.int32,(B,B),0)==lax.broadcasted_iota(jnp.int32,(B,B),1)
    zero=jnp.zeros((B,B),jnp.float32)
    for j in range(nj):
        u_ref[nb,j]=zero; l_ref[j,nb]=zero; a_ref[nb,j]=zero
    for j in range(nb):
        v_ref[nb,j]=zero; h_ref[j,nb]=zero
    for j in range(nb): s_ref[nb,j]=zero
    for ref in (ms_ref,ks_ref,mc_ref,kc_ref): ref[nb]=zero
    top=None
    for i in range(nb):
        for j in range(nj): a_ref[i,j]=ain_ref[i,j]
        for j in range(nb): s_ref[i,j]=sin_ref[i,j]
        d=jnp.where(eye,sin_ref[i,i],0.0)
        top=d if top is None else jnp.maximum(top,d)
    r0[...]=ain_ref[0,0]; r1[...]=sin_ref[0,0]
    def step(K,low):
        Kp=jnp.where(K==0,nb,K-1)
        tl=trail(a_ref,u_ref,l_ref,Kp,nb,nj); tc=trail(s_ref,v_ref,h_ref,Kp,nb,nb)
        def row0():
            put(ms_ref[Kp],ks_ref[Kp],[a_ref[Kp,j] for j in range(nj)],Kp,nb,u_ref,l_ref)
        def row1():
            put(mc_ref[Kp],kc_ref[Kp],[s_ref[Kp,j] for j in range(nb)],Kp,nb,v_ref,h_ref)
        def run(fs):
            for f in fs: f()
        half=len(tl)//2+1
        factor128([(r0,w0,k0,m0),(r1,w1,k1,m1)],
            [row0,functools.partial(run,[row1]+tl[:half]),functools.partial(run,tl[half:]+tc)])
        K1=jnp.minimum(K+1,nb-1)
        x0=mmul(m0[...],a_ref[K,K1]); x1=mmul(m1[...],s_ref[K,K1])
        r0[...]=a_ref[K1,K1]-mmul(x0.T,x0)
        r1[...]=s_ref[K1,K1]-mmul(x1.T,x1)
        ms_ref[K]=m0[...]; ks_ref[K]=k0[...]; mc_ref[K]=m1[...]; kc_ref[K]=k1[...]
        x=k1[...]
        return jnp.minimum(low,jnp.where(eye,x*x,1e30))
    low=lax.fori_loop(0,nb,step,jnp.full((B,B),1e30,jnp.float32))
    last=nb-1
    put(ms_ref[last],ks_ref[last],[a_ref[last,j] for j in range(nj)],last,nb,u_ref,l_ref)
    put(mc_ref[last],kc_ref[last],[s_ref[last,j] for j in range(nb)],last,nb,v_ref,h_ref)
    for i in range(no):
        for t in range(nb):
            chol_ref[i*B:(i+1)*B,t*B:(t+1)*B]=l_ref[nb+i,t]
    good=jnp.min(low)>=RATIO*jnp.max(top)
    @pl.when(good)
    def _():
        g=[]
        for K in range(nb):
            c=jnp.concatenate([h_ref[K,J] for J in range(K+1)],axis=1)
            for t in range(K):
                z=mmul(l_ref[K,t],g[t])
                c=jnp.concatenate([c[:,:(t+1)*B]-z,c[:,(t+1)*B:]],axis=1)
            g.append(mmul(ms_ref[K],c))
        for K in range(nb):
            for J in range(nb):
                prec_ref[K*B:(K+1)*B,J*B:(J+1)*B]=g[K][:,J*B:(J+1)*B] if J<=K else zero
    @pl.when(jnp.logical_not(good))
    def _():
        for C in range(nb):
            rows=[jnp.concatenate([u_ref[J,I] for I in range(C,nb)],axis=1) for J in range(C+1)]
            acc=mmul_nt(jnp.concatenate(rows,axis=0),rows[C])
            for J in range(C+1):
                v=acc[J*B:(J+1)*B]
                if J==C: v=v+jnp.where(eye,SHIFT,0.0)
                s_ref[J,C]=v
        for j in range(nb):
            v_ref[nb,j]=zero; h_ref[j,nb]=zero
        r1[...]=s_ref[0,0]
        def again(K,carry):
            Kp=jnp.where(K==0,nb,K-1)
            for f in trail(s_ref,v_ref,h_ref,Kp,nb,nb): f()
            factor128([(r1,w1,k1,m1)])
            put(m1[...],k1[...],[s_ref[K,j] for j in range(nb)],K,nb,v_ref,h_ref)
            K1=jnp.minimum(K+1,nb-1)
            r1[...]=s_ref[K1,K1]-mmul(h_ref[K1,K],v_ref[K,K1])
            return carry
        lax.fori_loop(0,nb,again,0)
        for J in range(nb):
            for C in range(nb):
                prec_ref[J*B:(J+1)*B,C*B:(C+1)*B]=h_ref[J,C]

def factor_kernel(a,s):
    nb,nj=a.shape[:2]; no=nj-nb
    vm=pl.BlockSpec(memory_space=pltpu.VMEM)
    f32=jnp.float32
    V=lambda *s: pltpu.VMEM(s+(B,B),f32)
    return pl.pallas_call(body,
        out_shape=(jax.ShapeDtypeStruct((no*B,nb*B),f32),jax.ShapeDtypeStruct((nb*B,nb*B),f32)),
        in_specs=[vm,vm],out_specs=(vm,vm),
        scratch_shapes=[V(nb+1,nj),V(nb+1,nj),V(nj,nb+1),V(nb+1,nb),V(nb+1,nb),V(nb,nb+1)]+[V(nb+1)]*4+[V()]*8,
        compiler_params=pltpu.CompilerParams(vmem_limit_bytes=24<<20),
        name='chol')(a,s)

def chol_kernel(off,panel,own):
    return factor_kernel(*init_kernel(off,panel,own))


LOG2E = 1.4426950408889634


def near(x):
    return pltpu.with_memory_space_constraint(x, pltpu.VMEM)


def far(x):
    return pltpu.with_memory_space_constraint(x, pltpu.HBM)


def load_body(c_hbm, s_hbm, c_ref, s_ref, sem, *, parts):
    copies = []
    for t, (src, dst) in enumerate([(c_hbm, c_ref)] + [(s_hbm, s_ref)] * parts):
        rows = src.shape[0] // (parts if t else 1)
        part = pl.ds((t - 1) * rows if t else 0, rows)
        copies.append(pltpu.make_async_copy(src.at[part], dst.at[part], sem.at[t]))
        copies[-1].start()
    for copy in copies:
        copy.wait()


def load_kernel(centers, samples, parts=2):
    outside = pl.BlockSpec(memory_space=pltpu.HBM)
    inside = pl.BlockSpec(memory_space=pltpu.VMEM)
    return pl.pallas_call(
        functools.partial(load_body, parts=parts),
        in_specs=[outside, outside],
        out_specs=(inside, inside),
        out_shape=(pltpu.VMEM(centers.shape, centers.dtype), pltpu.VMEM(samples.shape, samples.dtype)),
        scratch_shapes=[pltpu.SemaphoreType.DMA((1 + parts,))],
        compiler_params=pltpu.CompilerParams(vmem_limit_bytes=4 << 20),
        name="load",
    )(far(centers), far(samples))


def pair_body(other_ref, *refs):
    n = len(refs) // 2
    for d in range(n):
        refs[n + d][...] = refs[d][...] + other_ref[d]


def pair_kernel(other, mine):
    inside = pl.BlockSpec(memory_space=pltpu.VMEM)
    return pl.pallas_call(
        pair_body,
        in_specs=[inside] * (1 + len(mine)),
        out_specs=[inside] * len(mine),
        out_shape=[pltpu.VMEM(x.shape, x.dtype) for x in mine],
        compiler_params=pltpu.CompilerParams(vmem_limit_bytes=4 << 20),
        name="pair_sum",
    )(near(other), *[near(x) for x in mine])


def total_body(*refs, scale):
    total = refs[0][...]
    for ref in refs[1:-1]:
        total = total + ref[...]
    refs[-1][...] = total * scale


def total_kernel(parts, scale):
    inside = pl.BlockSpec(memory_space=pltpu.VMEM)
    return pl.pallas_call(
        functools.partial(total_body, scale=scale),
        in_specs=[inside] * len(parts),
        out_specs=inside,
        out_shape=jax.ShapeDtypeStruct(parts[0].shape, parts[0].dtype),
        compiler_params=pltpu.CompilerParams(vmem_limit_bytes=4 << 20),
        name="gram_sum",
    )(*[near(x) for x in parts])


def square_parts(x):
    sq = jnp.square(x.astype(jnp.float32))
    hi = sq.astype(jnp.bfloat16)
    return hi, (sq - hi.astype(jnp.float32)).astype(jnp.bfloat16)


def nt(a, b):
    return lax.dot_general(a, b, (((1,), (1,)), ((), ())), preferred_element_type=jnp.float32)


def row_norms(x, scale):
    hi, lo = square_parts(x)
    one = jnp.ones((8, x.shape[1]), jnp.bfloat16)
    return (nt(one, hi) + nt(one, lo))[0:1] * scale


def col_norms(x, scale):
    total = jnp.sum(jnp.square(x.astype(jnp.float32)), axis=1, keepdims=True) * scale
    return jnp.broadcast_to(total, (x.shape[0], B))


def kern_tile(x, y, xcol, yrow):
    dot = nt(x, y)
    both = jnp.concatenate([xcol] * (y.shape[0] // B), axis=1) + yrow
    arg = jnp.minimum(dot * (4.0 * LOG2E / x.shape[1]) + both, 0.0)
    return jnp.exp2(arg).astype(jnp.bfloat16)


def own_body(me_ref, c_ref, s_ref, k_ref, norm_ref, own_ref, *, row_dev):
    scale = -2.0 * LOG2E / c_ref.shape[1]
    at = pl.multiple_of(me_ref[0] * row_dev, row_dev)
    own_ref[0:row_dev, :] = c_ref[pl.ds(at, row_dev), :]
    if row_dev < own_ref.shape[0]:
        own_ref[row_dev:, :] = jnp.zeros((own_ref.shape[0] - row_dev, own_ref.shape[1]), own_ref.dtype)
    c = c_ref[...]
    ccol = col_norms(c, scale)
    tile = 2 * B
    for t in range(0, s_ref.shape[0], tile):
        s = s_ref[t : t + tile, :]
        norm_ref[t : t + tile, :] = col_norms(s, scale)
        k_ref[:, t : t + tile] = kern_tile(c, s, ccol, row_norms(s, scale))


def own_kernel(me, centers, samples, row_dev):
    mc, d = centers.shape
    ns = samples.shape[0]
    inside = pl.BlockSpec(memory_space=pltpu.VMEM)
    return pl.pallas_call(
        functools.partial(own_body, row_dev=row_dev),
        in_specs=[pl.BlockSpec(memory_space=pltpu.SMEM), inside, inside],
        out_specs=(inside, inside, inside),
        out_shape=(
            pltpu.VMEM((mc, ns), jnp.bfloat16),
            pltpu.VMEM((ns, B), jnp.float32),
            pltpu.VMEM((row_dev + -row_dev % B, d), jnp.bfloat16),
        ),
        compiler_params=pltpu.CompilerParams(vmem_limit_bytes=16 << 20),
        name="kern_own",
    )(me, centers, samples)


def gram_body(me_ref, *refs, samps, tile):
    pieces, (k_ref, s_ref, norm_ref) = refs[:samps], refs[samps : samps + 3]
    panel_ref, other_ref = refs[samps + 3 : samps + 5]
    mine, (acc_ref, kp_ref) = refs[samps + 5 : -2], refs[-2:]
    me = me_ref[0]
    rows = pieces[0].shape[0]
    for d in range(samps):
        panel_ref[pl.ds(pl.multiple_of((me ^ d) * rows, rows), rows), :] = pieces[d][...]
    panel = panel_ref[...]
    yrow = row_norms(panel, -2.0 * LOG2E / s_ref.shape[1])
    for t in range(0, s_ref.shape[0], tile):
        kp_ref[t : t + tile, :] = kern_tile(s_ref[t : t + tile, :], panel, norm_ref[t : t + tile, :], yrow)
    acc_ref[...] = jnp.dot(k_ref[...], kp_ref[...], preferred_element_type=jnp.float32)
    side = me & 1
    k = me >> 1
    rows = other_ref.shape[1]
    for d in range(samps // 2):
        at = (k ^ d) * 2
        mine[d][...] = acc_ref[pl.ds(pl.multiple_of((at + side) * rows, rows), rows), :]
        other_ref[d] = acc_ref[pl.ds(pl.multiple_of((at + 1 - side) * rows, rows), rows), :]


def gram_kernel(me, pieces, kern_own, samples, norms, tile=512):
    samps = len(pieces)
    mc, ns = kern_own.shape
    width = samps * pieces[0].shape[0]
    inside = pl.BlockSpec(memory_space=pltpu.VMEM)
    shape = (mc // samps, width)
    return pl.pallas_call(
        functools.partial(gram_body, samps=samps, tile=tile),
        in_specs=[pl.BlockSpec(memory_space=pltpu.SMEM)] + [inside] * (samps + 3),
        out_specs=(inside,) * (2 + samps // 2),
        out_shape=(
            pltpu.VMEM((width, samples.shape[1]), jnp.bfloat16),
            pltpu.VMEM((samps // 2,) + shape, jnp.float32),
        )
        + (pltpu.VMEM(shape, jnp.float32),) * (samps // 2),
        scratch_shapes=[pltpu.VMEM((mc, width), jnp.float32), pltpu.VMEM((ns, width), jnp.bfloat16)],
        compiler_params=pltpu.CompilerParams(vmem_limit_bytes=16 << 20),
        name="gram",
    )(me, *[near(x) for x in pieces], kern_own, samples, norms)


from jax.sharding import PartitionSpec as P

PANEL = 512
GRAM_SCALE = 64.0


def swap(x, axis, d):
    n = lax.axis_size(axis)
    return lax.ppermute(x, axis, [(i, i ^ d) for i in range(n)])


def panel_pieces(centers, samples):
    ctrs = lax.axis_size("ctr")
    samps = lax.axis_size("samp")
    rows = PANEL // samps
    chunk = lax.dynamic_slice_in_dim(centers, lax.axis_index("samp") * rows, rows, 0)
    got = [lax.ppermute(chunk, "ctr", [(0, d)]) for d in range(1, ctrs)]
    got, near_centers, near_samples = lax.optimization_barrier((got, *load_kernel(centers, samples)))
    total = got[0]
    for piece in got[1:]:
        total = total + piece
    chunk = jnp.where(lax.axis_index("ctr") == 0, chunk, total)
    return near_centers, near_samples, [chunk] + [swap(chunk, "samp", d) for d in range(1, samps)]


def local(samples, centers):
    samp_count = lax.axis_size("samp")
    samp_index = lax.axis_index("samp").astype(jnp.int32)
    ctr_index = lax.axis_index("ctr").astype(jnp.int32)
    mc_dev = centers.shape[0]
    row_dev = mc_dev // samp_count
    me = samp_index.reshape(1)
    near_centers, held, pieces = panel_pieces(centers, samples)
    kern_own, norms, own = own_kernel(me, near_centers, held, row_dev)
    panel, other, *mine = gram_kernel(me, pieces, kern_own, held, norms)
    other = swap(other, "samp", 1)
    off = (ctr_index * mc_dev + samp_index * row_dev).reshape(1)
    first, second = init_kernel(off, panel, own)
    other, first, second = lax.optimization_barrier((other, first, second))
    half = pair_kernel(other, mine)
    parts = [half[0]] + [swap(half[d], "samp", 2 * d) for d in range(1, samp_count // 2)]
    chol, precond = factor_kernel(first, second)
    gram = total_kernel(parts, GRAM_SCALE / (samples.shape[0] * samp_count))
    return (gram[None], chol[None, :row_dev], precond)


def solution(mesh):
    placed = (P("samp", None), P("ctr", None))
    return jax.shard_map(
        local,
        mesh=mesh,
        in_specs=placed,
        out_specs=(P("ctr", "samp", None), P("ctr", "samp", None), P()),
        check_vma=False,
    )
```
